128 devices in a mesh: lat: 8 (over y, core), lon: 16 (over z, x).
Axes of the slice: x: 4, y: 4, z: 4, core: 2. Of those that a mesh axis runs over, the one named last changes fastest.
Arguments:
- tracers: float32 [2, 4, 128, 4096], P(None, None, 'lat', 'lon'), may hold values from -6 to 6
- cotangent: float32 [2, 4, 128, 4096], P(None, None, 'lat', 'lon'), may hold values from -6 to 6
- land_mask: int32 [4, 128, 4096], P(None, 'lat', 'lon'), may hold values 0 or 1
- diffusion: float32 [3, 4, 128, 4096], P(None, None, 'lat', 'lon'), may hold values from 0.01 to 0.1
- velocity: float32 [2, 4, 128, 4096], P(None, None, 'lat', 'lon'), may hold values from -0.1 to 0.1
- weights: float32 [32, 128, 128], replicated, may hold values from -0.1875 to 0.1875
- atm_state: float32 [2, 8, 4096, 128], P(None, 'lat', 'lon'), may hold values from -6 to 6
- margins: int32 [3, 8, 16, 16, 64], P(None, 'lat', 'lon'), may hold values from -1 to 255, as said below
Outputs:
- final_tracers: float32 [2, 4, 128, 4096], P(None, None, 'lat', 'lon')
- adjoint_tracers: float32 [2, 4, 128, 4096], P(None, None, 'lat', 'lon')
- atm_gradient: float32 [2, 8, 4096, 128], P(None, 'lat', 'lon')
The draws below stay inside these ranges and needn't reach their ends.
Inputs may be any that keep to these rules, and one draw needn't show every extreme that they name: margins[0, i, j, k, s] is a top-level block of ocean tile (i, k), or -1 where slot s from longitude tile j to longitude tile k in latitude row i is empty; margins[1] is an atmosphere block of tile (i, j) and margins[2] a weight block in every slot. Live slots lie anywhere among the 64. In each latitude row one receiving tile has all 64 slots live from every sender.
All inputs are finite; a program needn't handle non-finite values. No bound on the sum of `land_mask` on one device may be relied on, other than what follows from the above.
Results may differ from the reference program's by a relative error of at most 0.0003.
Values sent between devices are 32-bit elements; how exact they have to be, the bound alone decides.
A program may use at most 64 MiB of HBM per device.

```python
import math
import jax
import jax.numpy as jnp
from jax import lax

LEV = 4
CLAT = 16
CLON = 256
BLOCK = 128
ATM_DEV = 256
CAP = 64
WBLOCKS = 32
STEPS = 4
LATS = 128
LONS = 4096
ATM_ROW = 4096
OCN_BLK = 32
N_LAT = 8
N_LON = 16


def draw_margins(key, part):
    keys = jax.random.split(key, 6)
    full_dest = jax.random.randint(keys[0], (N_LAT,), 0, N_LON)
    counts = jax.random.randint(keys[1], (N_LAT, N_LON, N_LON), 1, CAP // 2 + 1)
    dest_ids = jnp.arange(N_LON)[None, None, :]
    counts = jnp.where(dest_ids == full_dest[:, None, None], CAP, counts)
    scores = jax.random.randint(keys[2], (N_LAT, N_LON, N_LON, CAP), 0, 1 << 20) * CAP + jnp.arange(CAP)
    order = jnp.argsort(scores, axis=-1)
    ranks = jnp.argsort(order, axis=-1)
    live_slot = ranks < counts[..., None]
    ocean = jnp.where(live_slot, jax.random.randint(keys[3], (N_LAT, N_LON, N_LON, CAP), 0, OCN_BLK), -1)
    atmosphere = jax.random.randint(keys[4], (N_LAT, N_LON, N_LON, CAP), 0, ATM_DEV)
    table = jax.random.randint(keys[5], (N_LAT, N_LON, N_LON, CAP), 0, WBLOCKS)
    return jnp.stack([ocean, atmosphere, table]).astype(jnp.int32)


def place_ends(values, rng, least, top_value):
    index_at = [jax.random.randint(jax.random.fold_in(rng, axis), (), 0, length) for axis, length in enumerate(values.shape)]
    widest = values.shape.index(max(values.shape))
    neighbour = index_at[:widest] + [(index_at[widest] + 1) % values.shape[widest]] + index_at[widest + 1:]
    return values.at[tuple(index_at)].set(least).at[tuple(neighbour)].set(top_value)


def levels(own_key, extent, pieces, least, largest):
    gain, own = 1.0, jax.random.fold_in(own_key, 6)
    for axis_at, shards_of in pieces:
        heights = jnp.exp(jax.random.uniform(jax.random.fold_in(own, axis_at), (shards_of,), jnp.float32, least / len(pieces), largest / len(pieces)))
        gain = gain * jnp.repeat(heights, extent[axis_at] // shards_of).reshape([-1 if axis == axis_at else 1 for axis in range(len(extent))])
    return gain


def bell_draw(rng, shape, scale, limit, cuts=(), dtype=jnp.bfloat16):
    array = jax.random.normal(rng, shape, jnp.float32) * scale
    if len(cuts) > 0:
        array = levels(rng, shape, cuts, -0.22, 0.18) * array
    return jnp.clip(array, min=-limit, max=limit).astype(dtype)


def setup_inputs(seed: int = 0) -> dict:
    streams_of = jax.random.split(jax.random.key(seed), 9)
    return {
        "tracers": bell_draw(streams_of[0], (2, LEV, LATS, LONS), 1.0, 6.0, ((2, 8), (3, 16)), jnp.float32),
        "cotangent": bell_draw(streams_of[1], (2, LEV, LATS, LONS), 1.0, 6.0, ((2, 8), (3, 16)), jnp.float32),
        "land_mask": place_ends((jax.random.randint(streams_of[2], (LEV, LATS, LONS), 0, 5) < 4).astype(jnp.int32), jax.random.fold_in(streams_of[2], 1), 0, 1),
        "diffusion": jnp.clip(jnp.exp(math.log(0.1) - 2.3025851 * jax.random.uniform(streams_of[3], (3, LEV, LATS, LONS), jnp.float32) ** levels(streams_of[3], (3, LEV, LATS, LONS), ((2, 8), (3, 16)), -0.2, 0.2)), 0.01, 0.1),
        "velocity": jnp.clip(jax.random.uniform(streams_of[4], (2, LEV, LATS, LONS), jnp.float32, -0.1, 0.1) * levels(streams_of[4], (2, LEV, LATS, LONS), ((2, 8), (3, 16)), -0.4, 0.0), -0.1, 0.1),
        "weights": bell_draw(streams_of[5], (WBLOCKS, BLOCK, BLOCK), (8 * BLOCK) ** -0.5, 0.1875, (), jnp.float32),
        "atm_state": bell_draw(streams_of[6], (2, N_LAT, ATM_ROW, BLOCK), 1.0, 6.0, ((1, 8), (2, 16)), jnp.float32),
        "margins": draw_margins(jax.random.fold_in(streams_of[8], 71), 0),
    }


def face_terms(land_mask, diffusion, velocity):
    ocean_mask = land_mask.astype(jnp.float32)
    mask_east = jnp.roll(ocean_mask, -1, axis=2)
    mask_north = jnp.concatenate([ocean_mask[:, 1:], jnp.zeros_like(ocean_mask[:, :1])], axis=1)
    east_k = diffusion[0] * ocean_mask * mask_east
    east_v = velocity[0] * ocean_mask * mask_east
    north_k = diffusion[1] * ocean_mask * mask_north
    north_v = velocity[1] * ocean_mask * mask_north
    below_k = diffusion[2][:-1] * ocean_mask[:-1] * ocean_mask[1:]
    coeffs = (jnp.maximum(east_v, 0.0) + east_k, jnp.minimum(east_v, 0.0) - east_k, jnp.maximum(north_v, 0.0) + north_k, jnp.minimum(north_v, 0.0) - north_k, below_k)
    return (coeffs, ocean_mask)

def advance(quantity, coeffs):
    east_a, east_b, north_a, north_b, below_k = coeffs
    east_flux = east_a * quantity + east_b * jnp.roll(quantity, -1, axis=3)
    zero_row = jnp.zeros_like(quantity[:, :, :1])
    north_flux = north_a * quantity + north_b * jnp.concatenate([quantity[:, :, 1:], zero_row], axis=2)
    below_flux = below_k * (quantity[:, :-1] - quantity[:, 1:])
    zero_level = jnp.zeros_like(quantity[:, :1])
    return quantity - (east_flux - jnp.roll(east_flux, 1, axis=3)) - (north_flux - jnp.concatenate([zero_row, north_flux[:, :, :-1]], axis=2)) - (jnp.concatenate([below_flux, zero_level], axis=1) - jnp.concatenate([zero_level, below_flux], axis=1))

def slot_forcing(atm_state, weights, margins):

    def one_row(row_data):
        atm_row, slot_lists = row_data
        products = jnp.einsum('wpq,faq->wafp', weights, atm_row, precision=lax.Precision.HIGHEST)
        flat_table = products.reshape(WBLOCKS * ATM_ROW, 2 * BLOCK)
        source = jnp.arange(N_LON).astype(jnp.int32)[:, None, None]
        dest_ids = jnp.arange(N_LON).astype(jnp.int32)[None, :, None]
        table_rows = (slot_lists[2] * ATM_ROW + source * ATM_DEV + slot_lists[1]).astype(jnp.int32)
        values = jnp.take(flat_table, table_rows.reshape(-1), axis=0)
        target = jnp.where(slot_lists[0] >= 0, dest_ids * OCN_BLK + slot_lists[0], N_LON * OCN_BLK).astype(jnp.int32)
        block_sums = jax.ops.segment_sum(values, target.reshape(-1), num_segments=N_LON * OCN_BLK + 1)
        return block_sums[:-1]
    return lax.map(one_row, (atm_state.transpose(1, 0, 2, 3), margins.transpose(1, 0, 2, 3, 4)))

def slot_gradient(surface_blocks, weights, margins):

    def one_row(row_data):
        blocks_row, slot_lists = row_data
        source = jnp.arange(N_LON).astype(jnp.int32)[:, None, None]
        dest_ids = jnp.arange(N_LON).astype(jnp.int32)[None, :, None]
        live_slot = slot_lists[0] >= 0
        pick_rows = jnp.where(live_slot, dest_ids * OCN_BLK + slot_lists[0], 0).astype(jnp.int32)
        values = jnp.take(blocks_row, pick_rows.reshape(-1), axis=0) * live_slot.reshape(-1, 1).astype(jnp.float32)
        table_rows = (slot_lists[2] * ATM_ROW + source * ATM_DEV + slot_lists[1]).astype(jnp.int32)
        gathered = jax.ops.segment_sum(values, table_rows.reshape(-1), num_segments=WBLOCKS * ATM_ROW)
        gathered = gathered.reshape(WBLOCKS, ATM_ROW, 2, BLOCK)
        return jnp.einsum('wpq,wafp->faq', weights, gathered, precision=lax.Precision.HIGHEST)
    result = lax.map(one_row, (surface_blocks, margins.transpose(1, 0, 2, 3, 4)))
    return result.transpose(1, 0, 2, 3)

def blocks_to_field(blocks):
    shaped = blocks.reshape(N_LAT, N_LON, CLAT, CLON // BLOCK, 2, BLOCK)
    return shaped.transpose(4, 0, 2, 1, 3, 5).reshape(2, LATS, LONS)

def field_to_blocks(surface):
    shaped = surface.reshape(2, N_LAT, CLAT, N_LON, CLON // BLOCK, BLOCK)
    return shaped.transpose(1, 3, 2, 4, 0, 5).reshape(N_LAT, N_LON * OCN_BLK, 2 * BLOCK)

def reference(tracers, cotangent, land_mask, diffusion, velocity, weights, atm_state, margins):
    coeffs, ocean_mask = face_terms(land_mask, diffusion, velocity)
    surface = blocks_to_field(slot_forcing(atm_state, weights, margins)) * ocean_mask[0]
    force_full = jnp.concatenate([surface[:, None], jnp.zeros((2, LEV - 1, LATS, LONS), jnp.float32)], axis=1)
    quantity = tracers
    for step_index in range(STEPS):
        quantity = advance(quantity, coeffs) + force_full
    adjoint_map = jax.vjp(lambda inner: advance(inner, coeffs), jnp.zeros_like(cotangent))[1]
    adjoint = cotangent
    surface_sum = jnp.zeros_like(cotangent[:, 0])
    for step_index in range(STEPS):
        surface_sum = surface_sum + adjoint[:, 0]
        adjoint = adjoint_map(adjoint)[0]
    surface_adjoint = surface_sum * ocean_mask[0]
    gradient = slot_gradient(field_to_blocks(surface_adjoint), weights, margins)
    return (quantity, adjoint, gradient)
```

```python
import jax
import jax.numpy as jnp
from jax import lax
from jax.experimental import pallas as pl
from jax.experimental.pallas import tpu as pltpu
from jax.sharding import PartitionSpec as P

MESH = pl.DeviceIdType.MESH
F32 = jnp.float32
BF16 = jnp.bfloat16
BLOCK = 128
CAP = 64
STEPS = 4
LEV = 4
ROWS = 16
COLS = 256
XROWS = 24
XCOLS = 384
TRC, COT, DIF, VEL, MSK = 0, 8, 16, 28, 36
PLANES = 40
HALF = PLANES // 2
EA, EB, NA, NB, BK = 0, 4, 8, 12, 16
WB = 32
ATM = 256
OCN = 32
MSG = 2 * OCN
BATCH = 4


def iota(shape, axis):
    return lax.broadcasted_iota(jnp.int32, shape, axis)


def split(x):
    hi = x.astype(BF16)
    return hi, (x - hi.astype(F32)).astype(BF16)


def dot(a, b):
    return lax.dot_general(a, b, (((1,), (0,)), ((), ())), preferred_element_type=F32)


def dot_t(a, b):
    return lax.dot_general(a, b, (((1,), (1,)), ((), ())), preferred_element_type=F32)


def east(x):
    return pltpu.roll(x, XCOLS - 1, 1)


def west(x):
    return pltpu.roll(x, 1, 1)


def north(x):
    return pltpu.roll(x, XROWS - 1, 0)


def south(x):
    return pltpu.roll(x, 1, 0)


def kernel(
    n_lat, n_lon,
    tracers, cotangent, land, diffusion, velocity, weights, atm, slots_s, slots_v,
    out_t, out_c, out_g,
    ext, mask_i, atm_v, weights_v, coef, force, ssum,
    send_n, send_s, send_c, recv_n, recv_s, recv_e, recv_w, recv_d,
    fsend_r, fsend_c, frecv_n, frecv_s, frecv_e, frecv_w, frecv_d,
    w_fwd, w_rev, x_rows, x_cat, table_f, picked, p_send, p_recv,
    s_all, v_cat, table_r, z_rows, z_cat, ids, hot,
    load_sem, halo_send, halo_recv, p_ssem, p_rsem, s_ssem, s_rsem, f_send, f_recv, out_sem,
):
    lat, lon = lax.axis_index("lat"), lax.axis_index("lon")
    up, down = lax.rem(lat + 1, n_lat), lax.rem(lat + n_lat - 1, n_lat)
    right, left = lax.rem(lon + 1, n_lon), lax.rem(lon + n_lon - 1, n_lon)
    loads = [
        (tracers, ext.at[TRC : TRC + 8, 0:ROWS, 0:COLS]),
        (cotangent, ext.at[COT : COT + 8, 0:ROWS, 0:COLS]),
        (diffusion, ext.at[DIF : DIF + 12, 0:ROWS, 0:COLS]),
        (velocity, ext.at[VEL : VEL + 8, 0:ROWS, 0:COLS]),
        (land, mask_i),
        (atm, atm_v),
        (weights, weights_v),
    ]
    loads = [pltpu.make_async_copy(a, b, load_sem.at[i]) for i, (a, b) in enumerate(loads)]
    for copy in loads:
        copy.start()

    barrier = pltpu.get_barrier_semaphore()
    peers = [(up, lon), (down, lon), (up, left), (up, right), (down, left), (down, right)]
    for peer in peers:
        pl.semaphore_signal(barrier, inc=1, device_id=peer, device_id_type=MESH)

    @pl.loop(1, n_lon)
    def _(step):
        pl.semaphore_signal(barrier, inc=1, device_id=(lat, lax.rem(lon + step, n_lon)), device_id_type=MESH)

    pl.semaphore_wait(barrier, len(peers) + n_lon - 1)

    lane = iota((8, 128), 1)
    row = iota((8, 128), 0)
    row2 = iota((8, COLS), 0)
    low = row2 < 4
    group = lax.rem((lane + 4) // 8, 16)
    for copy in loads[:5]:
        copy.wait()
    ext[MSK : MSK + 4, 0:ROWS, 0:COLS] = mask_i[...].astype(F32)

    @pl.loop(0, HALF)
    def _(p):
        first, last = ext[p, 0:8, 0:COLS], ext[p, 8:16, 0:COLS]
        first2, last2 = ext[p + HALF, 0:8, 0:COLS], ext[p + HALF, 8:16, 0:COLS]
        send_n[p] = jnp.where(low, pltpu.roll(last2, 4, 0), last)
        send_s[p] = jnp.where(low, first, pltpu.roll(first2, 4, 0))

    def remote(src, dst, sems, i, peer):
        return pltpu.make_async_remote_copy(
            src_ref=src, dst_ref=dst, send_sem=sems[0].at[i], recv_sem=sems[1].at[i], device_id=peer, device_id_type=MESH
        )

    halo = (halo_send, halo_recv)
    halos = [remote(send_n, recv_s, halo, 0, (up, lon)), remote(send_s, recv_n, halo, 1, (down, lon))]
    for copy in halos:
        copy.start()

    def pack_columns(plane_of, count, put):
        for tile in range(-(-count // 16)):
            for r in (0, 8):
                acc = jnp.zeros((8, 128), F32)
                for q in range(min(16, count - 16 * tile)):
                    p = plane_of(16 * tile + q)
                    edge = jnp.where(lane < 4, p(r, 0), p(r, 128))
                    if q:
                        edge = pltpu.roll(edge, 8 * q, 1)
                    acc = jnp.where(group == q, edge, acc)
                put(r, tile, acc)

    def put_c(r, tile, value):
        send_c[r : r + 8, 128 * tile : 128 * tile + 128] = value

    pack_columns(lambda p: lambda r, c: ext[p, r : r + 8, c : c + 128], PLANES, put_c)

    def column_copies(src, to_e, to_w, to_d, sems, base):
        first, last = src.at[0:8], src.at[8:16]
        return [
            remote(src, to_w, sems, base, (lat, right)),
            remote(src, to_e, sems, base + 1, (lat, left)),
            remote(last, to_d.at[3], sems, base + 2, (up, right)),
            remote(last, to_d.at[1], sems, base + 3, (up, left)),
            remote(first, to_d.at[2], sems, base + 4, (down, right)),
            remote(first, to_d.at[0], sems, base + 5, (down, left)),
        ]

    columns = column_copies(send_c, recv_e, recv_w, recv_d, halo, 2)
    for copy in columns:
        copy.start()
    halos += columns

    for copy in loads[5:]:
        copy.wait()

    @pl.loop(0, WB // 2)
    def _(pair):
        for i in range(2):
            hi, lo = split(weights_v[2 * pair + i])
            w_fwd[pair, 128 * i : 128 * i + 128, 0:128] = hi
            w_fwd[pair, 128 * i : 128 * i + 128, 128:256] = lo
            w_rev[pair, 0:128, 128 * i : 128 * i + 128] = hi
            w_rev[pair, 128:256, 128 * i : 128 * i + 128] = lo

    for f in range(2):
        x_rows[pl.ds(f, ATM, stride=2), :] = atm_v[f]
    hi, lo = split(x_rows[...])
    x_cat[0 : 2 * ATM, 0:128] = hi
    x_cat[0 : 2 * ATM, 128:256] = hi
    x_cat[2 * ATM :, 0:128] = lo
    x_cat[2 * ATM :, 128:256] = lo

    @pl.loop(0, WB // 2)
    def _(pair):
        both = w_fwd[pair]
        out = dot_t(x_cat[0 : 2 * ATM], both) + dot_t(x_cat[2 * ATM :], both)
        at = pl.multiple_of(pair * (4 * ATM), 4 * ATM)
        table_f[pl.ds(at, 2 * ATM), :] = out[:, 0:128]
        table_f[pl.ds(at + 2 * ATM, 2 * ATM), :] = out[:, 128:256]

    for copy in halos:
        copy.wait_recv()

    edge_row = jnp.where(row < 4, (lat < n_lat - 1).astype(F32), (lat > 0).astype(F32))
    edge_row2 = jnp.where(low, (lat < n_lat - 1).astype(F32), (lat > 0).astype(F32))

    @pl.loop(0, HALF)
    def _(p):
        from_n, from_s = recv_n[p], recv_s[p]
        ext[p, 16:24, 0:COLS] = jnp.where(low, from_n, from_s)
        ext[p + HALF, 16:24, 0:COLS] = pltpu.roll(jnp.where(low, from_s, from_n), 4, 0)

    for p in range(MSK, MSK + 4):
        ext[p, 16:24, 0:COLS] = ext[p, 16:24, 0:COLS] * edge_row2

    from_east = lax.rem(lane, 8) < 4
    keep = jnp.logical_or(lane < 4, lane >= 124)

    def unpack_columns(from_e, from_w, from_d, count, put):
        for tile in range(-(-count // 16)):
            t = slice(128 * tile, 128 * tile + 128)
            for r in (0, 8, 16):
                if r < 16:
                    e, w = from_e[r : r + 8, t], from_w[r : r + 8, t]
                else:
                    e = jnp.where(row < 4, from_d[0, :, t], from_d[1, :, t])
                    w = jnp.where(row < 4, from_d[2, :, t], from_d[3, :, t])
                both = jnp.where(from_east, e, w)
                for q in range(min(16, count - 16 * tile)):
                    value = pltpu.roll(both, 128 - 8 * q, 1) if q else both
                    put(16 * tile + q, r, jnp.where(keep, value, 0.0))

    def put_x(p, r, value):
        if p >= MSK and r == 16:
            value = value * edge_row
        ext[p, r : r + 8, 256:384] = value

    unpack_columns(recv_e, recv_w, recv_d, PLANES, put_x)

    for lev in range(LEV):
        m = ext[MSK + lev]
        me, mn = m * east(m), m * north(m)
        k, v = ext[DIF + lev] * me, ext[VEL + lev] * me
        coef[EA + lev] = jnp.maximum(v, 0.0) + k
        coef[EB + lev] = jnp.minimum(v, 0.0) - k
        k, v = ext[DIF + LEV + lev] * mn, ext[VEL + LEV + lev] * mn
        coef[NA + lev] = jnp.maximum(v, 0.0) + k
        coef[NB + lev] = jnp.minimum(v, 0.0) - k
        if lev < LEV - 1:
            coef[BK + lev] = ext[DIF + 2 * LEV + lev] * m * ext[MSK + lev + 1]

    def retreat():
        for f in range(2):
            above = None
            for lev in range(LEV):
                p = COT + LEV * f + lev
                v = ext[p]
                step_x, step_y = east(v) - v, north(v) - v
                new = v + (coef[EA + lev] * step_x + west(coef[EB + lev] * step_x))
                new = new + (coef[NA + lev] * step_y + south(coef[NB + lev] * step_y))
                if lev < LEV - 1:
                    vertical = coef[BK + lev] * (ext[p + 1] - v)
                    new = new + vertical
                if above is not None:
                    new = new - above
                above = vertical
                ext[p] = new

    def advance():
        for f in range(2):
            above = None
            for lev in range(LEV):
                p = TRC + LEV * f + lev
                v = ext[p]
                flux_x = coef[EA + lev] * v + coef[EB + lev] * east(v)
                flux_y = coef[NA + lev] * v + coef[NB + lev] * north(v)
                new = v - (flux_x - west(flux_x)) - (flux_y - south(flux_y))
                if lev < LEV - 1:
                    below = coef[BK + lev] * (v - ext[p + 1])
                    new = new - below
                if above is not None:
                    new = new + above
                above = below
                if lev == 0:
                    new = new + force[f]
                ext[p] = new

    for f in range(2):
        ssum[f] = ext[COT + LEV * f, 0:ROWS, 0:COLS]

    @pl.loop(0, STEPS - 1)
    def _(step):
        retreat()
        for f in range(2):
            ssum[f] = ssum[f] + ext[COT + LEV * f, 0:ROWS, 0:COLS]

    mask0 = ext[MSK, 0:ROWS, 0:COLS]
    for f in range(2):
        surface = ssum[f] * mask0
        for h in range(2):
            s_all[lon, pl.ds(2 * h + f, ROWS, stride=4), :] = surface[:, 128 * h : 128 * h + 128]

    def surface_copy(step):
        return pltpu.make_async_remote_copy(
            src_ref=s_all.at[lon], dst_ref=s_all.at[lon], send_sem=s_ssem.at[step], recv_sem=s_rsem.at[step],
            device_id=(lat, lax.rem(lon + step, n_lon)), device_id_type=MESH,
        )

    @pl.loop(1, n_lon)
    def _(step):
        surface_copy(step).start()

    def partial(step):
        k = lax.rem(lon + step, n_lon)
        for s in range(CAP):
            at = slots_s[2, k, s] * (2 * ATM) + 2 * slots_s[1, k, s]
            picked[2 * s : 2 * s + 2, :] = table_f[pl.ds(at, 2), :]
        onehot = (slots_v[0, pl.ds(k, 1), :] == iota((OCN, CAP), 0)).astype(BF16)
        for f in range(2):
            hi, lo = split(picked[pl.ds(f, CAP, stride=2), :])
            p_send[step, pl.ds(f, OCN, stride=2), :] = dot(onehot, hi) + dot(onehot, lo)

    def partial_copy(step):
        return pltpu.make_async_remote_copy(
            src_ref=p_send.at[step], dst_ref=p_recv.at[step], send_sem=p_ssem.at[step], recv_sem=p_rsem.at[step],
            device_id=(lat, lax.rem(lon + step, n_lon)), device_id_type=MESH,
        )

    @pl.loop(1, n_lon)
    def _(step):
        partial(step)
        partial_copy(step).start()

    partial(0)
    retreat()
    adjoint_out = pltpu.make_async_copy(ext.at[COT : COT + 8, 0:ROWS, 0:COLS], out_c, out_sem.at[0])
    adjoint_out.start()

    def reverse(batch):
        for i in range(BATCH):
            step = batch * BATCH + i
            k = lax.rem(lon + n_lon - step, n_lon)
            hi, lo = split(s_all[k])
            v_cat[MSG * i : MSG * i + MSG, 0:128] = hi
            v_cat[MSG * i : MSG * i + MSG, 128:256] = hi
            v_cat[MSG * (BATCH + i) : MSG * (BATCH + i + 1), 0:128] = lo
            v_cat[MSG * (BATCH + i) : MSG * (BATCH + i + 1), 128:256] = lo
        size = MSG * BATCH

        @pl.loop(0, WB // 2)
        def _(pair):
            both = w_rev[pair]
            out = dot(v_cat[0:size], both) + dot(v_cat[size:], both)
            at = pl.multiple_of(pair * (2 * size), 2 * size)
            table_r[pl.ds(at, size), :] = out[:, 0:128]
            table_r[pl.ds(at + size, size), :] = out[:, 128:256]

        @pl.loop(0, BATCH)
        def _(i):
            k = lax.rem(lon + n_lon - (batch * BATCH + i), n_lon)
            base = pl.multiple_of(k * (2 * CAP), 2 * CAP)
            for s in range(CAP):
                at = slots_s[2, k, s] * size + i * MSG + 2 * jnp.maximum(slots_s[0, k, s], 0)
                z_rows[pl.ds(base + 2 * s, 2), :] = table_r[pl.ds(at, 2), :]

    def wait_surface(batch):
        for step in range(batch * BATCH, batch * BATCH + BATCH):
            if step:
                surface_copy(step).wait_recv()

    wait_surface(0)
    reverse(0)

    total = p_send[0]
    for step in range(1, 16):
        partial_copy(step).wait_recv()
        total = total + p_recv[step]
    p_send[0] = total
    for f in range(2):
        for h in range(2):
            part = p_send[0, pl.ds(2 * h + f, ROWS, stride=4), :]
            force[f, 0:ROWS, 128 * h : 128 * h + 128] = part * mask0[:, 128 * h : 128 * h + 128]
        fsend_r[f] = force[f, 0:ROWS, 0:COLS]

    fsem = (f_send, f_recv)

    def put_f(r, tile, value):
        fsend_c[r : r + 8, :] = value

    pack_columns(lambda p: lambda r, c: force[p, r : r + 8, c : c + 128], 2, put_f)
    fcopies = [
        remote(fsend_r.at[:, 8:16], frecv_s, fsem, 0, (up, lon)),
        remote(fsend_r.at[:, 0:8], frecv_n, fsem, 1, (down, lon)),
    ] + column_copies(fsend_c, frecv_e, frecv_w, frecv_d, fsem, 2)
    for copy in fcopies:
        copy.start()

    wait_surface(1)
    reverse(1)

    for copy in fcopies:
        copy.wait_recv()
    for f in range(2):
        force[f, 16:24, 0:COLS] = jnp.where(low, frecv_n[f], frecv_s[f]) * edge_row2

    def put_force(p, r, value):
        force[p, r : r + 8, 256:384] = value * edge_row if r == 16 else value

    unpack_columns(frecv_e, frecv_w, frecv_d, 2, put_force)

    @pl.loop(0, STEPS)
    def _(step):
        advance()

    tracer_out = pltpu.make_async_copy(ext.at[TRC : TRC + 8, 0:ROWS, 0:COLS], out_t, out_sem.at[1])
    tracer_out.start()

    for batch in range(2, 16 // BATCH):
        wait_surface(batch)
        reverse(batch)

    ids[:, 0:CAP] = jnp.where(slots_v[0] >= 0, slots_v[1], -1)
    for g in range(8):
        pick = jnp.concatenate([ids[2 * g : 2 * g + 1, 0:CAP], ids[2 * g + 1 : 2 * g + 2, 0:CAP]], axis=1)
        hot[:, 128 * g : 128 * g + 128] = (pick == iota((ATM, 128), 0)).astype(BF16)
    for f in range(2):
        hi, lo = split(z_rows[pl.ds(f, 16 * CAP, stride=2), :])
        z_cat[:, 128 * f : 128 * f + 128] = hi
        z_cat[:, 256 + 128 * f : 384 + 128 * f] = lo
    both = dot(hot[...], z_cat[:, 0:256]) + dot(hot[...], z_cat[:, 256:512])
    for f in range(2):
        out_g[f] = both[:, 128 * f : 128 * f + 128]

    for copy in halos + fcopies:
        copy.wait_send()

    @pl.loop(1, n_lon)
    def _(step):
        surface_copy(step).wait_send()
        partial_copy(step).wait_send()

    adjoint_out.wait()
    tracer_out.wait()


def on_device(n_lat, n_lon, tracers, cotangent, land_mask, diffusion, velocity, weights, atm_state, margins):
    fields = (2 * LEV, ROWS, COLS)
    margins = margins.reshape(3, n_lon, CAP)
    anywhere = pl.BlockSpec(memory_space=pl.ANY)
    vmem = pl.BlockSpec(memory_space=pltpu.VMEM)
    smem = pl.BlockSpec(memory_space=pltpu.SMEM)

    def buf(*shape, dtype=F32):
        return pltpu.VMEM(shape, dtype)

    dma = pltpu.SemaphoreType.DMA
    scratch = [
        buf(PLANES, XROWS, XCOLS), buf(LEV, ROWS, COLS, dtype=jnp.int32), buf(2, ATM, BLOCK), buf(WB, BLOCK, BLOCK),
        buf(20, XROWS, XCOLS), buf(2, XROWS, XCOLS), buf(2, ROWS, COLS),
        buf(HALF, 8, COLS), buf(HALF, 8, COLS), buf(ROWS, 384), buf(HALF, 8, COLS), buf(HALF, 8, COLS),
        buf(ROWS, 384), buf(ROWS, 384), buf(4, 8, 384),
        buf(2, ROWS, COLS), buf(ROWS, 128), buf(2, 8, COLS), buf(2, 8, COLS),
        buf(ROWS, 128), buf(ROWS, 128), buf(4, 8, 128),
        buf(WB // 2, 256, 256, dtype=BF16), buf(WB // 2, 256, 256, dtype=BF16), buf(2 * ATM, BLOCK),
        buf(4 * ATM, 256, dtype=BF16), buf(WB * 2 * ATM, BLOCK), buf(2 * CAP, BLOCK),
        buf(n_lon, MSG, BLOCK), buf(n_lon, MSG, BLOCK),
        buf(n_lon, MSG, BLOCK), buf(2 * BATCH * MSG, 256, dtype=BF16), buf(WB * BATCH * MSG, BLOCK),
        buf(n_lon * 2 * CAP, BLOCK), buf(n_lon * CAP, 512, dtype=BF16), buf(16, 128, dtype=jnp.int32),
        buf(ATM, n_lon * CAP, dtype=BF16),
        dma((7,)), dma((8,)), dma((8,)), dma((16,)), dma((16,)), dma((16,)), dma((16,)), dma((8,)), dma((8,)), dma((2,)),
    ]

    def body(*refs):
        kernel(n_lat, n_lon, *refs)

    out_t, out_c, out_g = pl.pallas_call(
        body,
        out_shape=(
            jax.ShapeDtypeStruct(fields, F32),
            jax.ShapeDtypeStruct(fields, F32),
            jax.ShapeDtypeStruct((2, ATM, BLOCK), F32),
        ),
        in_specs=[anywhere] * 7 + [smem, vmem],
        out_specs=(anywhere, anywhere, vmem),
        scratch_shapes=scratch,
        compiler_params=pltpu.CompilerParams(collective_id=0, has_side_effects=True, vmem_limit_bytes=48 << 20),
    )(
        tracers.reshape(fields),
        cotangent.reshape(fields),
        land_mask,
        diffusion.reshape(3 * LEV, ROWS, COLS),
        velocity.reshape(fields),
        weights,
        atm_state.reshape(2, ATM, BLOCK),
        margins,
        margins,
    )
    return out_t.reshape(tracers.shape), out_c.reshape(tracers.shape), out_g.reshape(atm_state.shape)


def solution(mesh):
    n_lat, n_lon = mesh.shape["lat"], mesh.shape["lon"]

    def run(*args):
        return on_device(n_lat, n_lon, *args)

    return jax.shard_map(
        run,
        mesh=mesh,
        in_specs=(
            P(None, None, "lat", "lon"),
            P(None, None, "lat", "lon"),
            P(None, "lat", "lon"),
            P(None, None, "lat", "lon"),
            P(None, None, "lat", "lon"),
            P(),
            P(None, "lat", "lon", None),
            P(None, "lat", "lon", None, None),
        ),
        out_specs=(
            P(None, None, "lat", "lon"),
            P(None, None, "lat", "lon"),
            P(None, "lat", "lon", None),
        ),
        check_vma=False,
    )
```

```python
import jax
import jax.numpy as jnp
from jax import lax
from jax.experimental import pallas as pl
from jax.experimental.pallas import tpu as pltpu
from jax.sharding import PartitionSpec as P

MESH = pl.DeviceIdType.MESH
F32 = jnp.float32
BF16 = jnp.bfloat16
BLOCK = 128
CAP = 64
STEPS = 4
LEV = 4
ROWS = 16
COLS = 256
XROWS = 24
XCOLS = 384
TRC, COT, DIF, VEL, MSK = 0, 8, 16, 28, 36
PLANES = 40
HALF = PLANES // 2
EA, EB, NA, NB, BK = 0, 4, 8, 12, 16
WB = 32
ATM = 256
OCN = 32
MSG = 2 * OCN
BATCH = 4


def iota(shape, axis):
    return lax.broadcasted_iota(jnp.int32, shape, axis)


def split(x):
    hi = x.astype(BF16)
    return hi, (x - hi.astype(F32)).astype(BF16)


def dot(a, b):
    return lax.dot_general(a, b, (((1,), (0,)), ((), ())), preferred_element_type=F32)


def dot_t(a, b):
    return lax.dot_general(a, b, (((1,), (1,)), ((), ())), preferred_element_type=F32)


def east(x):
    return pltpu.roll(x, XCOLS - 1, 1)


def west(x):
    return pltpu.roll(x, 1, 1)


def north(x):
    return pltpu.roll(x, XROWS - 1, 0)


def south(x):
    return pltpu.roll(x, 1, 0)


def kernel(
    n_lat, n_lon,
    tracers, cotangent, land, diffusion, velocity, weights, atm, margins,
    out_t, out_c, out_g,
    ext, mask_i, atm_v, weights_v, slots_s, slots_v, coef, force, ssum,
    send_n, send_s, send_c, recv_n, recv_s, recv_e, recv_w, recv_d,
    fsend_r, fsend_c, frecv_n, frecv_s, frecv_e, frecv_w, frecv_d,
    w_fwd, w_rev, x_rows, x_cat, table_f, picked, p_send, p_recv,
    s_all, v_cat, table_r, z_rows, z_cat, ids, hot, grad,
    load_sem, halo_send, halo_recv, p_ssem, p_rsem, s_ssem, s_rsem, f_send, f_recv, out_sem,
):
    lat, lon = lax.axis_index("lat"), lax.axis_index("lon")
    up, down = lax.rem(lat + 1, n_lat), lax.rem(lat + n_lat - 1, n_lat)
    right, left = lax.rem(lon + 1, n_lon), lax.rem(lon + n_lon - 1, n_lon)
    loads = [
        (tracers, ext.at[TRC : TRC + 8, 0:ROWS, 0:COLS]),
        (cotangent, ext.at[COT : COT + 8, 0:ROWS, 0:COLS]),
        (diffusion, ext.at[DIF : DIF + 12, 0:ROWS, 0:COLS]),
        (velocity, ext.at[VEL : VEL + 8, 0:ROWS, 0:COLS]),
        (land, mask_i),
        (atm, atm_v),
        (margins, slots_s),
        (margins, slots_v),
        (weights, weights_v),
    ]
    loads = [pltpu.make_async_copy(a, b, load_sem.at[i]) for i, (a, b) in enumerate(loads)]
    for copy in loads:
        copy.start()

    barrier = pltpu.get_barrier_semaphore()
    peers = [(up, lon), (down, lon), (up, left), (up, right), (down, left), (down, right)]
    for peer in peers:
        pl.semaphore_signal(barrier, inc=1, device_id=peer, device_id_type=MESH)

    @pl.loop(1, n_lon)
    def _(step):
        pl.semaphore_signal(barrier, inc=1, device_id=(lat, lax.rem(lon + step, n_lon)), device_id_type=MESH)

    pl.semaphore_wait(barrier, len(peers) + n_lon - 1)

    lane = iota((8, 128), 1)
    row = iota((8, 128), 0)
    row2 = iota((8, COLS), 0)
    low = row2 < 4
    group = lax.rem((lane + 4) // 8, 16)
    for copy in loads[:5]:
        copy.wait()
    ext[MSK : MSK + 4, 0:ROWS, 0:COLS] = mask_i[...].astype(F32)

    @pl.loop(0, HALF)
    def _(p):
        first, last = ext[p, 0:8, 0:COLS], ext[p, 8:16, 0:COLS]
        first2, last2 = ext[p + HALF, 0:8, 0:COLS], ext[p + HALF, 8:16, 0:COLS]
        send_n[p] = jnp.where(low, pltpu.roll(last2, 4, 0), last)
        send_s[p] = jnp.where(low, first, pltpu.roll(first2, 4, 0))

    def remote(src, dst, sems, i, peer):
        return pltpu.make_async_remote_copy(
            src_ref=src, dst_ref=dst, send_sem=sems[0].at[i], recv_sem=sems[1].at[i], device_id=peer, device_id_type=MESH
        )

    halo = (halo_send, halo_recv)
    halos = [remote(send_n, recv_s, halo, 0, (up, lon)), remote(send_s, recv_n, halo, 1, (down, lon))]
    for copy in halos:
        copy.start()

    def pack_columns(plane_of, count, put):
        for tile in range(-(-count // 16)):
            for r in (0, 8):
                acc = jnp.zeros((8, 128), F32)
                for q in range(min(16, count - 16 * tile)):
                    p = plane_of(16 * tile + q)
                    edge = jnp.where(lane < 4, p(r, 0), p(r, 128))
                    if q:
                        edge = pltpu.roll(edge, 8 * q, 1)
                    acc = jnp.where(group == q, edge, acc)
                put(r, tile, acc)

    def put_c(r, tile, value):
        send_c[r : r + 8, 128 * tile : 128 * tile + 128] = value

    pack_columns(lambda p: lambda r, c: ext[p, r : r + 8, c : c + 128], PLANES, put_c)

    def column_copies(src, to_e, to_w, to_d, sems, base):
        first, last = src.at[0:8], src.at[8:16]
        return [
            remote(src, to_w, sems, base, (lat, right)),
            remote(src, to_e, sems, base + 1, (lat, left)),
            remote(last, to_d.at[3], sems, base + 2, (up, right)),
            remote(last, to_d.at[1], sems, base + 3, (up, left)),
            remote(first, to_d.at[2], sems, base + 4, (down, right)),
            remote(first, to_d.at[0], sems, base + 5, (down, left)),
        ]

    columns = column_copies(send_c, recv_e, recv_w, recv_d, halo, 2)
    for copy in columns:
        copy.start()
    halos += columns

    for copy in loads[5:]:
        copy.wait()

    @pl.loop(0, WB // 2)
    def _(pair):
        for i in range(2):
            hi, lo = split(weights_v[2 * pair + i])
            w_fwd[pair, 128 * i : 128 * i + 128, 0:128] = hi
            w_fwd[pair, 128 * i : 128 * i + 128, 128:256] = lo
            w_rev[pair, 0:128, 128 * i : 128 * i + 128] = hi
            w_rev[pair, 128:256, 128 * i : 128 * i + 128] = lo

    for f in range(2):
        x_rows[pl.ds(f, ATM, stride=2), :] = atm_v[f]
    hi, lo = split(x_rows[...])
    x_cat[0 : 2 * ATM, 0:128] = hi
    x_cat[0 : 2 * ATM, 128:256] = hi
    x_cat[2 * ATM :, 0:128] = lo
    x_cat[2 * ATM :, 128:256] = lo

    @pl.loop(0, WB // 2, unroll=8)
    def _(pair):
        both = w_fwd[pair]
        out = dot_t(x_cat[0 : 2 * ATM], both) + dot_t(x_cat[2 * ATM :], both)
        at = pl.multiple_of(pair * (4 * ATM), 4 * ATM)
        table_f[pl.ds(at, 2 * ATM), :] = out[:, 0:128]
        table_f[pl.ds(at + 2 * ATM, 2 * ATM), :] = out[:, 128:256]

    def partial(step):
        k = lax.rem(lon + step, n_lon)
        for s in range(CAP):
            at = slots_s[2, k, s] * (2 * ATM) + 2 * slots_s[1, k, s]
            picked[2 * s : 2 * s + 2, :] = table_f[pl.ds(at, 2), :]
        onehot = (slots_v[0, pl.ds(k, 1), :] == iota((OCN, CAP), 0)).astype(BF16)
        for f in range(2):
            hi, lo = split(picked[pl.ds(f, CAP, stride=2), :])
            p_send[step, pl.ds(f, OCN, stride=2), :] = dot(onehot, hi) + dot(onehot, lo)

    def partial_copy(step):
        return pltpu.make_async_remote_copy(
            src_ref=p_send.at[step], dst_ref=p_recv.at[step], send_sem=p_ssem.at[step], recv_sem=p_rsem.at[step],
            device_id=(lat, lax.rem(lon + step, n_lon)), device_id_type=MESH,
        )

    @pl.loop(1, n_lon, unroll=5)
    def _(step):
        partial(step)
        partial_copy(step).start()

    partial(0)

    for copy in halos:
        copy.wait_recv()

    edge_row = jnp.where(row < 4, (lat < n_lat - 1).astype(F32), (lat > 0).astype(F32))
    edge_row2 = jnp.where(low, (lat < n_lat - 1).astype(F32), (lat > 0).astype(F32))

    @pl.loop(0, HALF)
    def _(p):
        from_n, from_s = recv_n[p], recv_s[p]
        ext[p, 16:24, 0:COLS] = jnp.where(low, from_n, from_s)
        ext[p + HALF, 16:24, 0:COLS] = pltpu.roll(jnp.where(low, from_s, from_n), 4, 0)

    for p in range(MSK, MSK + 4):
        ext[p, 16:24, 0:COLS] = ext[p, 16:24, 0:COLS] * edge_row2

    from_east = lax.rem(lane, 8) < 4
    keep = jnp.logical_or(lane < 4, lane >= 124)

    def unpack_columns(from_e, from_w, from_d, count, put):
        for tile in range(-(-count // 16)):
            t = slice(128 * tile, 128 * tile + 128)
            for r in (0, 8, 16):
                if r < 16:
                    e, w = from_e[r : r + 8, t], from_w[r : r + 8, t]
                else:
                    e = jnp.where(row < 4, from_d[0, :, t], from_d[1, :, t])
                    w = jnp.where(row < 4, from_d[2, :, t], from_d[3, :, t])
                both = jnp.where(from_east, e, w)
                for q in range(min(16, count - 16 * tile)):
                    value = pltpu.roll(both, 128 - 8 * q, 1) if q else both
                    put(16 * tile + q, r, jnp.where(keep, value, 0.0))

    def put_x(p, r, value):
        if p >= MSK and r == 16:
            value = value * edge_row
        ext[p, r : r + 8, 256:384] = value

    unpack_columns(recv_e, recv_w, recv_d, PLANES, put_x)

    for lev in range(LEV):
        m = ext[MSK + lev]
        me, mn = m * east(m), m * north(m)
        k, v = ext[DIF + lev] * me, ext[VEL + lev] * me
        coef[EA + lev] = jnp.maximum(v, 0.0) + k
        coef[EB + lev] = jnp.minimum(v, 0.0) - k
        k, v = ext[DIF + LEV + lev] * mn, ext[VEL + LEV + lev] * mn
        coef[NA + lev] = jnp.maximum(v, 0.0) + k
        coef[NB + lev] = jnp.minimum(v, 0.0) - k
        if lev < LEV - 1:
            coef[BK + lev] = ext[DIF + 2 * LEV + lev] * m * ext[MSK + lev + 1]

    def retreat():
        for f in range(2):
            above = None
            for lev in range(LEV):
                p = COT + LEV * f + lev
                v = ext[p]
                step_x, step_y = east(v) - v, north(v) - v
                new = v + (coef[EA + lev] * step_x + west(coef[EB + lev] * step_x))
                new = new + (coef[NA + lev] * step_y + south(coef[NB + lev] * step_y))
                if lev < LEV - 1:
                    vertical = coef[BK + lev] * (ext[p + 1] - v)
                    new = new + vertical
                if above is not None:
                    new = new - above
                above = vertical
                ext[p] = new

    def advance():
        for f in range(2):
            above = None
            for lev in range(LEV):
                p = TRC + LEV * f + lev
                v = ext[p]
                flux_x = coef[EA + lev] * v + coef[EB + lev] * east(v)
                flux_y = coef[NA + lev] * v + coef[NB + lev] * north(v)
                new = v - (flux_x - west(flux_x)) - (flux_y - south(flux_y))
                if lev < LEV - 1:
                    below = coef[BK + lev] * (v - ext[p + 1])
                    new = new - below
                if above is not None:
                    new = new + above
                above = below
                if lev == 0:
                    new = new + force[f]
                ext[p] = new

    for f in range(2):
        ssum[f] = ext[COT + LEV * f, 0:ROWS, 0:COLS]

    @pl.loop(0, STEPS - 1)
    def _(step):
        retreat()
        for f in range(2):
            ssum[f] = ssum[f] + ext[COT + LEV * f, 0:ROWS, 0:COLS]

    mask0 = ext[MSK, 0:ROWS, 0:COLS]
    for f in range(2):
        surface = ssum[f] * mask0
        for h in range(2):
            s_all[lon, pl.ds(2 * h + f, ROWS, stride=4), :] = surface[:, 128 * h : 128 * h + 128]

    def surface_copy(step):
        return pltpu.make_async_remote_copy(
            src_ref=s_all.at[lon], dst_ref=s_all.at[lon], send_sem=s_ssem.at[step], recv_sem=s_rsem.at[step],
            device_id=(lat, lax.rem(lon + step, n_lon)), device_id_type=MESH,
        )

    @pl.loop(1, n_lon)
    def _(step):
        surface_copy(step).start()

    retreat()
    adjoint_out = pltpu.make_async_copy(ext.at[COT : COT + 8, 0:ROWS, 0:COLS], out_c, out_sem.at[0])
    adjoint_out.start()

    def reverse(batch):
        for i in range(BATCH):
            step = batch * BATCH + i
            k = lax.rem(lon + n_lon - step, n_lon)
            hi, lo = split(s_all[k])
            v_cat[MSG * i : MSG * i + MSG, 0:128] = hi
            v_cat[MSG * i : MSG * i + MSG, 128:256] = hi
            v_cat[MSG * (BATCH + i) : MSG * (BATCH + i + 1), 0:128] = lo
            v_cat[MSG * (BATCH + i) : MSG * (BATCH + i + 1), 128:256] = lo
        size = MSG * BATCH

        @pl.loop(0, WB // 2, unroll=8)
        def _(pair):
            both = w_rev[pair]
            out = dot(v_cat[0:size], both) + dot(v_cat[size:], both)
            at = pl.multiple_of(pair * (2 * size), 2 * size)
            table_r[pl.ds(at, size), :] = out[:, 0:128]
            table_r[pl.ds(at + size, size), :] = out[:, 128:256]

        @pl.loop(0, BATCH)
        def _(i):
            k = lax.rem(lon + n_lon - (batch * BATCH + i), n_lon)
            base = pl.multiple_of(i * (2 * CAP), 2 * CAP)
            for s in range(CAP):
                at = slots_s[2, k, s] * size + i * MSG + 2 * jnp.maximum(slots_s[0, k, s], 0)
                z_rows[pl.ds(base + 2 * s, 2), :] = table_r[pl.ds(at, 2), :]

        for i in range(BATCH):
            k = lax.rem(lon + n_lon - (batch * BATCH + i), n_lon)
            live = slots_v[0, pl.ds(k, 1), :] >= 0
            ids[i : i + 1, 0:CAP] = jnp.where(live, slots_v[1, pl.ds(k, 1), :], -1)
        for g in range(BATCH // 2):
            pick = jnp.concatenate([ids[2 * g : 2 * g + 1, 0:CAP], ids[2 * g + 1 : 2 * g + 2, 0:CAP]], axis=1)
            hot[:, 128 * g : 128 * g + 128] = (pick == iota((ATM, 128), 0)).astype(BF16)
        for f in range(2):
            hi, lo = split(z_rows[pl.ds(f, BATCH * CAP, stride=2), :])
            z_cat[:, 128 * f : 128 * f + 128] = hi
            z_cat[:, 256 + 128 * f : 384 + 128 * f] = lo
        part = dot(hot[...], z_cat[:, 0:256]) + dot(hot[...], z_cat[:, 256:512])
        for f in range(2):
            grad[f] = part[:, 128 * f : 128 * f + 128] + (grad[f] if batch else 0.0)

    def wait_surface(batch):
        for step in range(batch * BATCH, batch * BATCH + BATCH):
            if step:
                surface_copy(step).wait_recv()

    wait_surface(0)
    reverse(0)

    total = p_send[0]
    for step in range(1, 16):
        partial_copy(step).wait_recv()
        total = total + p_recv[step]
    p_send[0] = total
    for f in range(2):
        for h in range(2):
            part = p_send[0, pl.ds(2 * h + f, ROWS, stride=4), :]
            force[f, 0:ROWS, 128 * h : 128 * h + 128] = part * mask0[:, 128 * h : 128 * h + 128]
        fsend_r[f] = force[f, 0:ROWS, 0:COLS]

    fsem = (f_send, f_recv)

    def put_f(r, tile, value):
        fsend_c[r : r + 8, :] = value

    pack_columns(lambda p: lambda r, c: force[p, r : r + 8, c : c + 128], 2, put_f)
    fcopies = [
        remote(fsend_r.at[:, 8:16], frecv_s, fsem, 0, (up, lon)),
        remote(fsend_r.at[:, 0:8], frecv_n, fsem, 1, (down, lon)),
    ] + column_copies(fsend_c, frecv_e, frecv_w, frecv_d, fsem, 2)
    for copy in fcopies:
        copy.start()

    wait_surface(1)
    reverse(1)

    for copy in fcopies:
        copy.wait_recv()
    for f in range(2):
        force[f, 16:24, 0:COLS] = jnp.where(low, frecv_n[f], frecv_s[f]) * edge_row2

    def put_force(p, r, value):
        force[p, r : r + 8, 256:384] = value * edge_row if r == 16 else value

    unpack_columns(frecv_e, frecv_w, frecv_d, 2, put_force)

    @pl.loop(0, STEPS)
    def _(step):
        advance()

    tracer_out = pltpu.make_async_copy(ext.at[TRC : TRC + 8, 0:ROWS, 0:COLS], out_t, out_sem.at[1])
    tracer_out.start()

    for batch in range(2, 16 // BATCH):
        wait_surface(batch)
        reverse(batch)

    grad_out = pltpu.make_async_copy(grad, out_g, out_sem.at[2])
    grad_out.start()

    for copy in halos + fcopies:
        copy.wait_send()

    @pl.loop(1, n_lon)
    def _(step):
        surface_copy(step).wait_send()
        partial_copy(step).wait_send()

    adjoint_out.wait()
    tracer_out.wait()
    grad_out.wait()


def on_device(n_lat, n_lon, tracers, cotangent, land_mask, diffusion, velocity, weights, atm_state, margins):
    fields = (2 * LEV, ROWS, COLS)
    margins = margins.reshape(3, n_lon, CAP)
    anywhere = pl.BlockSpec(memory_space=pltpu.HBM)

    def buf(*shape, dtype=F32):
        return pltpu.VMEM(shape, dtype)

    dma = pltpu.SemaphoreType.DMA
    scratch = [
        buf(PLANES, XROWS, XCOLS), buf(LEV, ROWS, COLS, dtype=jnp.int32), buf(2, ATM, BLOCK), buf(WB, BLOCK, BLOCK),
        pltpu.SMEM((3, n_lon, CAP), jnp.int32), buf(3, n_lon, CAP, dtype=jnp.int32),
        buf(20, XROWS, XCOLS), buf(2, XROWS, XCOLS), buf(2, ROWS, COLS),
        buf(HALF, 8, COLS), buf(HALF, 8, COLS), buf(ROWS, 384), buf(HALF, 8, COLS), buf(HALF, 8, COLS),
        buf(ROWS, 384), buf(ROWS, 384), buf(4, 8, 384),
        buf(2, ROWS, COLS), buf(ROWS, 128), buf(2, 8, COLS), buf(2, 8, COLS),
        buf(ROWS, 128), buf(ROWS, 128), buf(4, 8, 128),
        buf(WB // 2, 256, 256, dtype=BF16), buf(WB // 2, 256, 256, dtype=BF16), buf(2 * ATM, BLOCK),
        buf(4 * ATM, 256, dtype=BF16), buf(WB * 2 * ATM, BLOCK), buf(2 * CAP, BLOCK),
        buf(n_lon, MSG, BLOCK), buf(n_lon, MSG, BLOCK),
        buf(n_lon, MSG, BLOCK), buf(2 * BATCH * MSG, 256, dtype=BF16), buf(WB * BATCH * MSG, BLOCK),
        buf(BATCH * 2 * CAP, BLOCK), buf(BATCH * CAP, 512, dtype=BF16), buf(16, 128, dtype=jnp.int32),
        buf(ATM, BATCH * CAP, dtype=BF16), buf(2, ATM, BLOCK),
        dma((9,)), dma((8,)), dma((8,)), dma((16,)), dma((16,)), dma((16,)), dma((16,)), dma((8,)), dma((8,)), dma((3,)),
    ]

    def body(*refs):
        kernel(n_lat, n_lon, *refs)

    out_t, out_c, out_g = pl.pallas_call(
        body,
        out_shape=(
            jax.ShapeDtypeStruct(fields, F32),
            jax.ShapeDtypeStruct(fields, F32),
            jax.ShapeDtypeStruct((2, ATM, BLOCK), F32),
        ),
        in_specs=[anywhere] * 8,
        out_specs=(anywhere, anywhere, anywhere),
        scratch_shapes=scratch,
        compiler_params=pltpu.CompilerParams(collective_id=0, has_side_effects=True, vmem_limit_bytes=48 << 20),
    )(*(pltpu.with_memory_space_constraint(x, pltpu.HBM) for x in (
        tracers.reshape(fields),
        cotangent.reshape(fields),
        land_mask,
        diffusion.reshape(3 * LEV, ROWS, COLS),
        velocity.reshape(fields),
        weights,
        atm_state.reshape(2, ATM, BLOCK),
        margins,
    )))
    return out_t.reshape(tracers.shape), out_c.reshape(tracers.shape), out_g.reshape(atm_state.shape)


def solution(mesh):
    n_lat, n_lon = mesh.shape["lat"], mesh.shape["lon"]

    def run(*args):
        return on_device(n_lat, n_lon, *args)

    return jax.shard_map(
        run,
        mesh=mesh,
        in_specs=(
            P(None, None, "lat", "lon"),
            P(None, None, "lat", "lon"),
            P(None, "lat", "lon"),
            P(None, None, "lat", "lon"),
            P(None, None, "lat", "lon"),
            P(),
            P(None, "lat", "lon", None),
            P(None, "lat", "lon", None, None),
        ),
        out_specs=(
            P(None, None, "lat", "lon"),
            P(None, None, "lat", "lon"),
            P(None, "lat", "lon", None),
        ),
        check_vma=False,
    )
```

```python
import jax
import jax.numpy as jnp
from jax import lax
from jax.experimental import pallas as pl
from jax.experimental.pallas import tpu as pltpu
from jax.sharding import PartitionSpec as P

MESH = pl.DeviceIdType.MESH
F32 = jnp.float32
BF16 = jnp.bfloat16
BLOCK = 128
CAP = 64
STEPS = 4
LEV = 4
ROWS = 16
COLS = 256
XROWS = 24
XCOLS = 384
TRC, COT, DIF, VEL, MSK = 0, 8, 16, 28, 36
PLANES = 40
HALF = PLANES // 2
EA, EB, NA, NB, BK = 0, 4, 8, 12, 16
WB = 32
ATM = 256
OCN = 32
MSG = 2 * OCN
PLANE_ORDER = (0, 1, 3, 2)
BATCH = 4


def iota(shape, axis):
    return lax.broadcasted_iota(jnp.int32, shape, axis)


def split(x):
    hi = x.astype(BF16)
    return hi, (x - hi.astype(F32)).astype(BF16)


def dot(a, b):
    return lax.dot_general(a, b, (((1,), (0,)), ((), ())), preferred_element_type=F32)


def dot_t(a, b):
    return lax.dot_general(a, b, (((1,), (1,)), ((), ())), preferred_element_type=F32)


def east(x):
    return pltpu.roll(x, XCOLS - 1, 1)


def west(x):
    return pltpu.roll(x, 1, 1)


def north(x):
    return pltpu.roll(x, XROWS - 1, 0)


def south(x):
    return pltpu.roll(x, 1, 0)


def kernel(
    n_lat, n_lon,
    tracers, cotangent, land, diffusion, velocity, weights, atm, margins,
    out_t, out_c, out_g,
    ext, mask_i, atm_v, weights_v, slots_s, slots_v, coef, force, ssum,
    send_n, send_s, send_c, recv_n, recv_s, recv_e, recv_w, recv_d,
    fsend_r, fsend_c, frecv_n, frecv_s, frecv_e, frecv_w, frecv_d,
    w_fwd, w_rev, x_rows, x_cat, table_f, picked, p_send, p_recv,
    s_all, v_cat, table_r, z_rows, ids, hot, hot_o, grad,
    load_sem, halo_send, halo_recv, p_ssem, p_rsem, s_ssem, s_rsem, f_send, f_recv, out_sem,
):
    lat, lon = lax.axis_index("lat"), lax.axis_index("lon")
    up, down = lax.rem(lat + 1, n_lat), lax.rem(lat + n_lat - 1, n_lat)
    right, left = lax.rem(lon + 1, n_lon), lax.rem(lon + n_lon - 1, n_lon)
    loads = [
        (tracers, ext.at[TRC : TRC + 8, 0:ROWS, 0:COLS]),
        (cotangent, ext.at[COT : COT + 8, 0:ROWS, 0:COLS]),
        (diffusion, ext.at[DIF : DIF + 12, 0:ROWS, 0:COLS]),
        (velocity, ext.at[VEL : VEL + 8, 0:ROWS, 0:COLS]),
        (land, mask_i),
        (atm, atm_v),
        (margins, slots_s),
        (margins, slots_v),
        (weights, weights_v),
    ]
    loads = [pltpu.make_async_copy(a, b, load_sem.at[i]) for i, (a, b) in enumerate(loads)]
    for copy in loads:
        copy.start()

    barrier = pltpu.get_barrier_semaphore()
    peers = [(up, lon), (down, lon), (up, left), (up, right), (down, left), (down, right)]
    for peer in peers:
        pl.semaphore_signal(barrier, inc=1, device_id=peer, device_id_type=MESH)

    @pl.loop(1, n_lon)
    def _(step):
        pl.semaphore_signal(barrier, inc=1, device_id=(lat, lax.rem(lon + step, n_lon)), device_id_type=MESH)

    plane, place = lax.div(lon, 4), lax.rem(lon, 4)

    def target(step):
        return 4 * lax.rem(plane + lax.div(step, 4), 4) + lax.rem(place + lax.rem(step, 4), 4)

    def source(step):
        return 4 * lax.rem(plane + 4 - lax.div(step, 4), 4) + lax.rem(place + 4 - lax.rem(step, 4), 4)

    lane = iota((8, 128), 1)
    row = iota((8, 128), 0)
    row2 = iota((8, COLS), 0)
    low = row2 < 4
    group = lax.rem((lane + 4) // 8, 16)
    for copy in loads[:5]:
        copy.wait()
    ext[MSK : MSK + 4, 0:ROWS, 0:COLS] = mask_i[...].astype(F32)

    @pl.loop(0, HALF)
    def _(p):
        first, last = ext[p, 0:8, 0:COLS], ext[p, 8:16, 0:COLS]
        first2, last2 = ext[p + HALF, 0:8, 0:COLS], ext[p + HALF, 8:16, 0:COLS]
        send_n[p] = jnp.where(low, pltpu.roll(last2, 4, 0), last)
        send_s[p] = jnp.where(low, first, pltpu.roll(first2, 4, 0))

    def remote(src, dst, sems, i, peer):
        return pltpu.make_async_remote_copy(
            src_ref=src, dst_ref=dst, send_sem=sems[0].at[i], recv_sem=sems[1].at[i], device_id=peer, device_id_type=MESH
        )

    def pack_columns(plane_of, count, put):
        for tile in range(-(-count // 16)):
            for r in (0, 8):
                acc = jnp.zeros((8, 128), F32)
                for q in range(min(16, count - 16 * tile)):
                    p = plane_of(16 * tile + q)
                    edge = jnp.where(lane < 4, p(r, 0), p(r, 128))
                    if q:
                        edge = pltpu.roll(edge, 8 * q, 1)
                    acc = jnp.where(group == q, edge, acc)
                put(r, tile, acc)

    def put_c(r, tile, value):
        send_c[r : r + 8, 128 * tile : 128 * tile + 128] = value

    pack_columns(lambda p: lambda r, c: ext[p, r : r + 8, c : c + 128], PLANES, put_c)

    def column_copies(src, to_e, to_w, to_d, sems, base):
        first, last = src.at[0:8], src.at[8:16]
        return [
            remote(src, to_w, sems, base, (lat, right)),
            remote(src, to_e, sems, base + 1, (lat, left)),
            remote(last, to_d.at[3], sems, base + 2, (up, right)),
            remote(last, to_d.at[1], sems, base + 3, (up, left)),
            remote(first, to_d.at[2], sems, base + 4, (down, right)),
            remote(first, to_d.at[0], sems, base + 5, (down, left)),
        ]

    pl.semaphore_wait(barrier, len(peers) + n_lon - 1)

    halo = (halo_send, halo_recv)
    halos = [remote(send_n, recv_s, halo, 0, (up, lon)), remote(send_s, recv_n, halo, 1, (down, lon))]
    for copy in halos:
        copy.start()

    columns = column_copies(send_c, recv_e, recv_w, recv_d, halo, 2)
    for copy in columns:
        copy.start()
    halos += columns

    for copy in loads[5:]:
        copy.wait()

    @pl.loop(0, WB // 2)
    def _(pair):
        for i in range(2):
            hi, lo = split(weights_v[2 * pair + i])
            w_fwd[pair, 128 * i : 128 * i + 128, 0:128] = hi
            w_fwd[pair, 128 * i : 128 * i + 128, 128:256] = lo
            w_rev[pair, 0:128, 128 * i : 128 * i + 128] = hi
            w_rev[pair, 128:256, 128 * i : 128 * i + 128] = lo

    for f in range(2):
        x_rows[pl.ds(f, ATM, stride=2), :] = atm_v[f]
    hi, lo = split(x_rows[...])
    x_cat[0 : 2 * ATM, 0:128] = hi
    x_cat[0 : 2 * ATM, 128:256] = hi
    x_cat[2 * ATM :, 0:128] = lo
    x_cat[2 * ATM :, 128:256] = lo

    @pl.loop(0, WB // 2, unroll=8)
    def _(pair):
        both = w_fwd[pair]
        out = dot_t(x_cat[0 : 2 * ATM], both) + dot_t(x_cat[2 * ATM :], both)
        at = pl.multiple_of(pair * (4 * ATM), 4 * ATM)
        table_f[pl.ds(at, 2 * ATM), :] = out[:, 0:128]
        table_f[pl.ds(at + 2 * ATM, 2 * ATM), :] = out[:, 128:256]

    ids[:, 0:CAP] = jnp.where(slots_v[0] >= 0, slots_v[1], -1)

    @pl.loop(0, n_lon, unroll=4)
    def _(step):
        k = target(step)
        onehot = (slots_v[0, pl.ds(k, 1), :] == iota((OCN, CAP), 0)).astype(BF16)
        hot_o[step, :, 0:CAP] = onehot
        hot_o[step, :, CAP:] = onehot

    def partial(step):
        k = target(step)
        for s in range(CAP):
            at = slots_s[2, k, s] * (2 * ATM) + 2 * slots_s[1, k, s]
            picked[2 * s : 2 * s + 2, :] = table_f[pl.ds(at, 2), :]
        terms = [split(picked[pl.ds(f, CAP, stride=2), :]) for f in range(2)]
        rhs = jnp.concatenate([jnp.concatenate([t[i] for t in terms], axis=1) for i in range(2)], axis=0)
        sums = dot(hot_o[step], rhs)
        for f in range(2):
            p_send[step, pl.ds(f, OCN, stride=2), :] = sums[:, 128 * f : 128 * f + 128]

    def partial_copy(step):
        return pltpu.make_async_remote_copy(
            src_ref=p_send.at[step], dst_ref=p_recv.at[step], send_sem=p_ssem.at[step], recv_sem=p_rsem.at[step],
            device_id=(lat, target(step)), device_id_type=MESH,
        )

    @pl.loop(1, n_lon, unroll=5)
    def _(step):
        partial(step)
        partial_copy(step).start()

    partial(0)

    for copy in halos:
        copy.wait_recv()

    edge_row = jnp.where(row < 4, (lat < n_lat - 1).astype(F32), (lat > 0).astype(F32))
    edge_row2 = jnp.where(low, (lat < n_lat - 1).astype(F32), (lat > 0).astype(F32))

    @pl.loop(0, HALF)
    def _(p):
        from_n, from_s = recv_n[p], recv_s[p]
        ext[p, 16:24, 0:COLS] = jnp.where(low, from_n, from_s)
        ext[p + HALF, 16:24, 0:COLS] = pltpu.roll(jnp.where(low, from_s, from_n), 4, 0)

    for p in range(MSK, MSK + 4):
        ext[p, 16:24, 0:COLS] = ext[p, 16:24, 0:COLS] * edge_row2

    from_east = lax.rem(lane, 8) < 4
    keep = jnp.logical_or(lane < 4, lane >= 124)

    def unpack_columns(from_e, from_w, from_d, count, put):
        for tile in range(-(-count // 16)):
            t = slice(128 * tile, 128 * tile + 128)
            for r in (0, 8, 16):
                if r < 16:
                    e, w = from_e[r : r + 8, t], from_w[r : r + 8, t]
                else:
                    e = jnp.where(row < 4, from_d[0, :, t], from_d[1, :, t])
                    w = jnp.where(row < 4, from_d[2, :, t], from_d[3, :, t])
                both = jnp.where(from_east, e, w)
                for q in range(min(16, count - 16 * tile)):
                    value = pltpu.roll(both, 128 - 8 * q, 1) if q else both
                    put(16 * tile + q, r, jnp.where(keep, value, 0.0))

    def put_x(p, r, value):
        if p >= MSK and r == 16:
            value = value * edge_row
        ext[p, r : r + 8, 256:384] = value

    unpack_columns(recv_e, recv_w, recv_d, PLANES, put_x)

    for lev in range(LEV):
        m = ext[MSK + lev]
        me, mn = m * east(m), m * north(m)
        k, v = ext[DIF + lev] * me, ext[VEL + lev] * me
        coef[EA + lev] = jnp.maximum(v, 0.0) + k
        coef[EB + lev] = jnp.minimum(v, 0.0) - k
        k, v = ext[DIF + LEV + lev] * mn, ext[VEL + LEV + lev] * mn
        coef[NA + lev] = jnp.maximum(v, 0.0) + k
        coef[NB + lev] = jnp.minimum(v, 0.0) - k
        if lev < LEV - 1:
            coef[BK + lev] = ext[DIF + 2 * LEV + lev] * m * ext[MSK + lev + 1]

    def retreat():
        for f in range(2):
            above = None
            for lev in range(LEV):
                p = COT + LEV * f + lev
                v = ext[p]
                step_x, step_y = east(v) - v, north(v) - v
                new = v + (coef[EA + lev] * step_x + west(coef[EB + lev] * step_x))
                new = new + (coef[NA + lev] * step_y + south(coef[NB + lev] * step_y))
                if lev < LEV - 1:
                    vertical = coef[BK + lev] * (ext[p + 1] - v)
                    new = new + vertical
                if above is not None:
                    new = new - above
                above = vertical
                ext[p] = new

    def advance():
        for f in range(2):
            above = None
            for lev in range(LEV):
                p = TRC + LEV * f + lev
                v = ext[p]
                flux_x = coef[EA + lev] * v + coef[EB + lev] * east(v)
                flux_y = coef[NA + lev] * v + coef[NB + lev] * north(v)
                new = v - (flux_x - west(flux_x)) - (flux_y - south(flux_y))
                if lev < LEV - 1:
                    below = coef[BK + lev] * (v - ext[p + 1])
                    new = new - below
                if above is not None:
                    new = new + above
                above = below
                if lev == 0:
                    new = new + force[f]
                ext[p] = new

    for f in range(2):
        ssum[f] = ext[COT + LEV * f, 0:ROWS, 0:COLS]

    @pl.loop(0, STEPS - 1)
    def _(step):
        retreat()
        for f in range(2):
            ssum[f] = ssum[f] + ext[COT + LEV * f, 0:ROWS, 0:COLS]

    mask0 = ext[MSK, 0:ROWS, 0:COLS]
    for f in range(2):
        surface = ssum[f] * mask0
        for h in range(2):
            s_all[lon, pl.ds(2 * h + f, ROWS, stride=4), :] = surface[:, 128 * h : 128 * h + 128]

    def surface_copy(step):
        return pltpu.make_async_remote_copy(
            src_ref=s_all.at[lon], dst_ref=s_all.at[lon], send_sem=s_ssem.at[step], recv_sem=s_rsem.at[step],
            device_id=(lat, target(step)), device_id_type=MESH,
        )

    def send_surface(batch):
        for step in range(BATCH * PLANE_ORDER[batch], BATCH * PLANE_ORDER[batch] + BATCH):
            if step:
                surface_copy(step).start()

    send_surface(0)
    send_surface(1)

    for g in range(16 // 2):
        first, second = (source(BATCH * PLANE_ORDER[2 * g // BATCH] + 2 * g % BATCH + i) for i in range(2))
        pick = jnp.concatenate([ids[pl.ds(first, 1), 0:CAP], ids[pl.ds(second, 1), 0:CAP]], axis=1)
        hot[:, 128 * g : 128 * g + 128] = (pick == iota((ATM, 128), 0)).astype(BF16)

    retreat()
    adjoint_out = pltpu.make_async_copy(ext.at[COT : COT + 8, 0:ROWS, 0:COLS], out_c, out_sem.at[0])
    adjoint_out.start()

    def reverse(batch):
        for i in range(BATCH):
            hi, lo = split(s_all[source(BATCH * PLANE_ORDER[batch] + i)])
            v_cat[MSG * i : MSG * i + MSG, 0:128] = hi
            v_cat[MSG * i : MSG * i + MSG, 128:256] = hi
            v_cat[MSG * (BATCH + i) : MSG * (BATCH + i + 1), 0:128] = lo
            v_cat[MSG * (BATCH + i) : MSG * (BATCH + i + 1), 128:256] = lo
        size = MSG * BATCH

        @pl.loop(0, WB // 2, unroll=8)
        def _(pair):
            both = w_rev[pair]
            out = dot(v_cat[0:size], both) + dot(v_cat[size:], both)
            at = pl.multiple_of(pair * (2 * size), 2 * size)
            table_r[pl.ds(at, size), :] = out[:, 0:128]
            table_r[pl.ds(at + size, size), :] = out[:, 128:256]

        @pl.loop(0, BATCH)
        def _(i):
            k = source(BATCH * PLANE_ORDER[batch] + i)
            base = pl.multiple_of(i * (2 * CAP), 2 * CAP)
            for s in range(CAP):
                at = slots_s[2, k, s] * size + i * MSG + 2 * jnp.maximum(slots_s[0, k, s], 0)
                z_rows[pl.ds(base + 2 * s, 2), :] = table_r[pl.ds(at, 2), :]

        terms = [split(z_rows[pl.ds(f, BATCH * CAP, stride=2), :]) for f in range(2)]
        rhs = jnp.concatenate([jnp.concatenate([t[i] for t in terms], axis=1) for i in range(2)], axis=0)
        chosen = hot[:, BATCH * CAP * batch : BATCH * CAP * (batch + 1)]
        part = dot(jnp.concatenate([chosen, chosen], axis=1), rhs)
        for f in range(2):
            grad[f] = part[:, 128 * f : 128 * f + 128] + (grad[f] if batch else 0.0)

    def wait_surface(batch):
        for step in range(BATCH * PLANE_ORDER[batch], BATCH * PLANE_ORDER[batch] + BATCH):
            if step:
                surface_copy(step).wait_recv()

    wait_surface(0)
    send_surface(2)
    reverse(0)
    total = p_send[0]
    for step in range(1, 16):
        partial_copy(step).wait_recv()
        total = total + p_recv[step]
    p_send[0] = total
    for f in range(2):
        for h in range(2):
            part = p_send[0, pl.ds(2 * h + f, ROWS, stride=4), :]
            force[f, 0:ROWS, 128 * h : 128 * h + 128] = part * mask0[:, 128 * h : 128 * h + 128]
        fsend_r[f] = force[f, 0:ROWS, 0:COLS]

    fsem = (f_send, f_recv)

    def put_f(r, tile, value):
        fsend_c[r : r + 8, :] = value

    pack_columns(lambda p: lambda r, c: force[p, r : r + 8, c : c + 128], 2, put_f)
    fcopies = [
        remote(fsend_r.at[:, 8:16], frecv_s, fsem, 0, (up, lon)),
        remote(fsend_r.at[:, 0:8], frecv_n, fsem, 1, (down, lon)),
    ] + column_copies(fsend_c, frecv_e, frecv_w, frecv_d, fsem, 2)
    for copy in fcopies:
        copy.start()

    wait_surface(1)
    send_surface(3)
    reverse(1)
    wait_surface(2)
    reverse(2)

    wait_surface(3)
    reverse(3)

    grad_out = pltpu.make_async_copy(grad, out_g, out_sem.at[2])
    grad_out.start()

    for copy in fcopies:
        copy.wait_recv()
    for f in range(2):
        force[f, 16:24, 0:COLS] = jnp.where(low, frecv_n[f], frecv_s[f]) * edge_row2

    def put_force(p, r, value):
        force[p, r : r + 8, 256:384] = value * edge_row if r == 16 else value

    unpack_columns(frecv_e, frecv_w, frecv_d, 2, put_force)

    @pl.loop(0, STEPS)
    def _(step):
        advance()

    tracer_out = pltpu.make_async_copy(ext.at[TRC : TRC + 8, 0:ROWS, 0:COLS], out_t, out_sem.at[1])
    tracer_out.start()

    for copy in halos + fcopies:
        copy.wait_send()

    @pl.loop(1, n_lon)
    def _(step):
        surface_copy(step).wait_send()
        partial_copy(step).wait_send()

    adjoint_out.wait()
    tracer_out.wait()
    grad_out.wait()


def place(a, b, c, out_a, out_b, out_c, sem):
    copies = [pltpu.make_async_copy(x, y, sem.at[i]) for i, (x, y) in enumerate(((a, out_a), (b, out_b), (c, out_c)))]
    for copy in copies:
        copy.start()
    for copy in copies:
        copy.wait()


def on_device(n_lat, n_lon, tracers, cotangent, land_mask, diffusion, velocity, weights, atm_state, margins):
    fields = (2 * LEV, ROWS, COLS)
    margins = margins.reshape(3, n_lon, CAP)
    anywhere = pl.BlockSpec(memory_space=pltpu.HBM)

    def buf(*shape, dtype=F32):
        return pltpu.VMEM(shape, dtype)

    dma = pltpu.SemaphoreType.DMA
    scratch = [
        buf(PLANES, XROWS, XCOLS), buf(LEV, ROWS, COLS, dtype=jnp.int32), buf(2, ATM, BLOCK), buf(WB, BLOCK, BLOCK),
        pltpu.SMEM((3, n_lon, CAP), jnp.int32), buf(3, n_lon, CAP, dtype=jnp.int32),
        buf(20, XROWS, XCOLS), buf(2, XROWS, XCOLS), buf(2, ROWS, COLS),
        buf(HALF, 8, COLS), buf(HALF, 8, COLS), buf(ROWS, 384), buf(HALF, 8, COLS), buf(HALF, 8, COLS),
        buf(ROWS, 384), buf(ROWS, 384), buf(4, 8, 384),
        buf(2, ROWS, COLS), buf(ROWS, 128), buf(2, 8, COLS), buf(2, 8, COLS),
        buf(ROWS, 128), buf(ROWS, 128), buf(4, 8, 128),
        buf(WB // 2, 256, 256, dtype=BF16), buf(WB // 2, 256, 256, dtype=BF16), buf(2 * ATM, BLOCK),
        buf(4 * ATM, 256, dtype=BF16), buf(WB * 2 * ATM, BLOCK), buf(2 * CAP, BLOCK),
        buf(n_lon, MSG, BLOCK), buf(n_lon, MSG, BLOCK),
        buf(n_lon, MSG, BLOCK), buf(2 * BATCH * MSG, 256, dtype=BF16), buf(WB * BATCH * MSG, BLOCK),
        buf(BATCH * 2 * CAP, BLOCK), buf(16, 128, dtype=jnp.int32),
        buf(ATM, n_lon * CAP, dtype=BF16), buf(n_lon, OCN, 2 * CAP, dtype=BF16), buf(2, ATM, BLOCK),
        dma((9,)), dma((8,)), dma((8,)), dma((16,)), dma((16,)), dma((16,)), dma((16,)), dma((8,)), dma((8,)), dma((3,)),
    ]

    def body(*refs):
        kernel(n_lat, n_lon, *refs)

    out_t, out_c, out_g = pl.pallas_call(
        body,
        out_shape=(
            jax.ShapeDtypeStruct(fields, F32),
            jax.ShapeDtypeStruct(fields, F32),
            jax.ShapeDtypeStruct((2, ATM, BLOCK), F32),
        ),
        in_specs=[anywhere] * 8,
        out_specs=(anywhere, anywhere, anywhere),
        scratch_shapes=scratch,
        compiler_params=pltpu.CompilerParams(collective_id=0, has_side_effects=True, vmem_limit_bytes=48 << 20),
    )(*(pltpu.with_memory_space_constraint(x, pltpu.HBM) for x in (
        tracers.reshape(fields),
        cotangent.reshape(fields),
        land_mask,
        diffusion.reshape(3 * LEV, ROWS, COLS),
        velocity.reshape(fields),
        weights,
        atm_state.reshape(2, ATM, BLOCK),
        margins,
    )))
    out_t, out_c, out_g = pl.pallas_call(
        place,
        out_shape=(
            jax.ShapeDtypeStruct(fields, F32),
            jax.ShapeDtypeStruct(fields, F32),
            jax.ShapeDtypeStruct((2, ATM, BLOCK), F32),
        ),
        in_specs=[pl.BlockSpec(memory_space=pltpu.VMEM)] * 3,
        compiler_params=pltpu.CompilerParams(vmem_limit_bytes=2 << 20),
        out_specs=(anywhere,) * 3,
        scratch_shapes=[dma((3,))],
    )(out_t, out_c, out_g)
    return out_t.reshape(tracers.shape), out_c.reshape(tracers.shape), out_g.reshape(atm_state.shape)


def solution(mesh):
    n_lat, n_lon = mesh.shape["lat"], mesh.shape["lon"]

    def run(*args):
        return on_device(n_lat, n_lon, *args)

    return jax.shard_map(
        run,
        mesh=mesh,
        in_specs=(
            P(None, None, "lat", "lon"),
            P(None, None, "lat", "lon"),
            P(None, "lat", "lon"),
            P(None, None, "lat", "lon"),
            P(None, None, "lat", "lon"),
            P(),
            P(None, "lat", "lon", None),
            P(None, "lat", "lon", None, None),
        ),
        out_specs=(
            P(None, None, "lat", "lon"),
            P(None, None, "lat", "lon"),
            P(None, "lat", "lon", None),
        ),
        check_vma=False,
    )
```

```python
import jax
import jax.numpy as jnp
from jax import lax
from jax.experimental import pallas as pl
from jax.experimental.pallas import tpu as pltpu
from jax.sharding import PartitionSpec as P

MESH = pl.DeviceIdType.MESH
F32 = jnp.float32
BF16 = jnp.bfloat16
BLOCK = 128
CAP = 64
STEPS = 4
LEV = 4
ROWS = 16
COLS = 256
XROWS = 24
XCOLS = 384
TRC, COT, DIF, VEL, MSK = 0, 8, 16, 28, 36
PLANES = 40
HALF = PLANES // 2
EA, EB, NA, NB, BK = 0, 4, 8, 12, 16
WB = 32
ATM = 256
OCN = 32
MSG = 2 * OCN
PLANE_ORDER = (0, 1, 3, 2)
BATCH = 4


def iota(shape, axis):
    return lax.broadcasted_iota(jnp.int32, shape, axis)


def split(x):
    hi = x.astype(BF16)
    return hi, (x - hi.astype(F32)).astype(BF16)


def dot(a, b):
    return lax.dot_general(a, b, (((1,), (0,)), ((), ())), preferred_element_type=F32)


def dot_t(a, b):
    return lax.dot_general(a, b, (((1,), (1,)), ((), ())), preferred_element_type=F32)


def east(x):
    return pltpu.roll(x, XCOLS - 1, 1)


def west(x):
    return pltpu.roll(x, 1, 1)


def north(x):
    return pltpu.roll(x, XROWS - 1, 0)


def south(x):
    return pltpu.roll(x, 1, 0)


def kernel(
    n_lat, n_lon,
    tracers, cotangent, land, diffusion, velocity, weights, atm, margins,
    out_t, out_c, out_g,
    ext, mask_i, atm_v, weights_v, rows_s, rows_v, slots_v, coef, force, ssum,
    send_n, send_s, send_c, recv_n, recv_s, recv_e, recv_w, recv_d,
    fsend_r, fsend_c, frecv_n, frecv_s, frecv_e, frecv_w, frecv_d,
    w_fwd, w_rev, x_rows, x_cat, table_f, picked, p_send, p_recv, q_send, q_recv,
    s_all, v_cat, table_r, z_rows, ids, hot, hot_o, grad,
    load_sem, halo_send, halo_recv, p_ssem, p_rsem, s_ssem, s_rsem, f_send, f_recv, out_sem,
):
    lat, lon = lax.axis_index("lat"), lax.axis_index("lon")
    up, down = lax.rem(lat + 1, n_lat), lax.rem(lat + n_lat - 1, n_lat)
    right, left = lax.rem(lon + 1, n_lon), lax.rem(lon + n_lon - 1, n_lon)
    loads = [
        (tracers, ext.at[TRC : TRC + 8, 0:ROWS, 0:COLS]),
        (cotangent, ext.at[COT : COT + 8, 0:ROWS, 0:COLS]),
        (diffusion, ext.at[DIF : DIF + 12, 0:ROWS, 0:COLS]),
        (velocity, ext.at[VEL : VEL + 8, 0:ROWS, 0:COLS]),
        (land, mask_i),
        (margins, slots_v),
        (atm, atm_v),
        (weights, weights_v),
    ]
    loads = [pltpu.make_async_copy(a, b, load_sem.at[i]) for i, (a, b) in enumerate(loads)]
    for copy in loads:
        copy.start()

    barrier = pltpu.get_barrier_semaphore()
    plane, place = lax.div(lon, 4), lax.rem(lon, 4)

    def in_plane(b):
        return (lat, 4 * plane + lax.rem(place + b, 4))

    def across(a):
        return (lat, 4 * lax.rem(plane + a, 4) + place)

    peers = [(up, lon), (down, lon), (up, left), (up, right), (down, left), (down, right), (lat, left), (lat, right)]
    peers += [in_plane(i) for i in range(1, 4)] + [across(i) for i in range(1, 4)]
    for peer in peers:
        pl.semaphore_signal(barrier, inc=1, device_id=peer, device_id_type=MESH)


    def target(step):
        return 4 * lax.rem(plane + lax.div(step, 4), 4) + lax.rem(place + lax.rem(step, 4), 4)

    def source(step):
        return 4 * lax.rem(plane + 4 - lax.div(step, 4), 4) + lax.rem(place + 4 - lax.rem(step, 4), 4)

    lane = iota((8, 128), 1)
    row = iota((8, 128), 0)
    row2 = iota((8, COLS), 0)
    low = row2 < 4
    group = lax.rem((lane + 4) // 8, 16)
    for copy in loads[:6]:
        copy.wait()
    ext[MSK : MSK + 4, 0:ROWS, 0:COLS] = mask_i[...].astype(F32)

    @pl.loop(0, HALF)
    def _(p):
        first, last = ext[p, 0:8, 0:COLS], ext[p, 8:16, 0:COLS]
        first2, last2 = ext[p + HALF, 0:8, 0:COLS], ext[p + HALF, 8:16, 0:COLS]
        send_n[p] = jnp.where(low, pltpu.roll(last2, 4, 0), last)
        send_s[p] = jnp.where(low, first, pltpu.roll(first2, 4, 0))

    def remote(src, dst, sems, i, peer):
        return pltpu.make_async_remote_copy(
            src_ref=src, dst_ref=dst, send_sem=sems[0].at[i], recv_sem=sems[1].at[i], device_id=peer, device_id_type=MESH
        )

    ids[:, 0:CAP] = jnp.where(slots_v[0] >= 0, slots_v[1], -1)
    rows_v[0, :, 0:CAP] = slots_v[2] * (2 * ATM) + 2 * slots_v[1]
    rows_v[1, :, 0:CAP] = slots_v[2] * (MSG * BATCH) + 2 * jnp.maximum(slots_v[0], 0)
    index_copy = pltpu.make_async_copy(rows_v, rows_s, load_sem.at[8])
    index_copy.start()

    def pack_columns(plane_of, count, put):
        for tile in range(-(-count // 16)):
            for r in (0, 8):
                acc = jnp.zeros((8, 128), F32)
                for q in range(min(16, count - 16 * tile)):
                    p = plane_of(16 * tile + q)
                    edge = jnp.where(lane < 4, p(r, 0), p(r, 128))
                    if q:
                        edge = pltpu.roll(edge, 8 * q, 1)
                    acc = jnp.where(group == q, edge, acc)
                put(r, tile, acc)

    def put_c(r, tile, value):
        send_c[r : r + 8, 128 * tile : 128 * tile + 128] = value

    pack_columns(lambda p: lambda r, c: ext[p, r : r + 8, c : c + 128], PLANES, put_c)

    def column_copies(src, to_e, to_w, to_d, sems, base):
        first, last = src.at[0:8], src.at[8:16]
        return [
            remote(src, to_w, sems, base, (lat, right)),
            remote(src, to_e, sems, base + 1, (lat, left)),
            remote(last, to_d.at[3], sems, base + 2, (up, right)),
            remote(last, to_d.at[1], sems, base + 3, (up, left)),
            remote(first, to_d.at[2], sems, base + 4, (down, right)),
            remote(first, to_d.at[0], sems, base + 5, (down, left)),
        ]

    pl.semaphore_wait(barrier, len(peers))

    halo = (halo_send, halo_recv)
    halos = [remote(send_n, recv_s, halo, 0, (up, lon)), remote(send_s, recv_n, halo, 1, (down, lon))]
    for copy in halos:
        copy.start()

    columns = column_copies(send_c, recv_e, recv_w, recv_d, halo, 2)
    for copy in columns:
        copy.start()
    halos += columns

    for copy in loads[6:]:
        copy.wait()
    index_copy.wait()

    @pl.loop(0, WB // 2)
    def _(pair):
        for i in range(2):
            hi, lo = split(weights_v[2 * pair + i])
            w_fwd[pair, 128 * i : 128 * i + 128, 0:128] = hi
            w_fwd[pair, 128 * i : 128 * i + 128, 128:256] = lo
            w_rev[pair, 0:128, 128 * i : 128 * i + 128] = hi
            w_rev[pair, 128:256, 128 * i : 128 * i + 128] = lo

    for f in range(2):
        x_rows[pl.ds(f, ATM, stride=2), :] = atm_v[f]
    hi, lo = split(x_rows[...])
    x_cat[0 : 2 * ATM, 0:128] = hi
    x_cat[0 : 2 * ATM, 128:256] = hi
    x_cat[2 * ATM :, 0:128] = lo
    x_cat[2 * ATM :, 128:256] = lo

    @pl.loop(0, WB // 2, unroll=8)
    def _(pair):
        both = w_fwd[pair]
        out = dot_t(x_cat[0 : 2 * ATM], both) + dot_t(x_cat[2 * ATM :], both)
        at = pl.multiple_of(pair * (4 * ATM), 4 * ATM)
        table_f[pl.ds(at, 2 * ATM), :] = out[:, 0:128]
        table_f[pl.ds(at + 2 * ATM, 2 * ATM), :] = out[:, 128:256]


    @pl.loop(0, n_lon, unroll=4)
    def _(step):
        k = target(step)
        onehot = (slots_v[0, pl.ds(k, 1), :] == iota((OCN, CAP), 0)).astype(BF16)
        hot_o[step, :, 0:CAP] = onehot
        hot_o[step, :, CAP:] = onehot

    def partial(step):
        k = target(step)
        for s in range(CAP):
            at = rows_s[0, k, s]
            picked[2 * s : 2 * s + 2, :] = table_f[pl.ds(at, 2), :]
        terms = [split(picked[pl.ds(f, CAP, stride=2), :]) for f in range(2)]
        rhs = jnp.concatenate([jnp.concatenate([t[i] for t in terms], axis=1) for i in range(2)], axis=0)
        sums = dot(hot_o[step], rhs)
        for f in range(2):
            p_send[step, pl.ds(f, OCN, stride=2), :] = sums[:, 128 * f : 128 * f + 128]

    psem = (p_ssem, p_rsem)

    partials = [remote(p_send.at[4 * a : 4 * a + 4], p_recv.at[4 * a : 4 * a + 4], psem, a - 1, across(a)) for a in range(1, 4)]
    for a in (1, 3, 2):
        pl.loop(4 * a, 4 * a + 4, unroll=4)(partial)
        partials[a - 1].start()
    pl.loop(0, 4, unroll=4)(partial)

    for copy in halos:
        copy.wait_recv()

    edge_row = jnp.where(row < 4, (lat < n_lat - 1).astype(F32), (lat > 0).astype(F32))
    edge_row2 = jnp.where(low, (lat < n_lat - 1).astype(F32), (lat > 0).astype(F32))

    @pl.loop(0, HALF)
    def _(p):
        from_n, from_s = recv_n[p], recv_s[p]
        ext[p, 16:24, 0:COLS] = jnp.where(low, from_n, from_s)
        ext[p + HALF, 16:24, 0:COLS] = pltpu.roll(jnp.where(low, from_s, from_n), 4, 0)

    for p in range(MSK, MSK + 4):
        ext[p, 16:24, 0:COLS] = ext[p, 16:24, 0:COLS] * edge_row2

    from_east = lax.rem(lane, 8) < 4
    keep = jnp.logical_or(lane < 4, lane >= 124)

    def unpack_columns(from_e, from_w, from_d, count, put):
        for tile in range(-(-count // 16)):
            t = slice(128 * tile, 128 * tile + 128)
            for r in (0, 8, 16):
                if r < 16:
                    e, w = from_e[r : r + 8, t], from_w[r : r + 8, t]
                else:
                    e = jnp.where(row < 4, from_d[0, :, t], from_d[1, :, t])
                    w = jnp.where(row < 4, from_d[2, :, t], from_d[3, :, t])
                both = jnp.where(from_east, e, w)
                for q in range(min(16, count - 16 * tile)):
                    value = pltpu.roll(both, 128 - 8 * q, 1) if q else both
                    put(16 * tile + q, r, jnp.where(keep, value, 0.0))

    def put_x(p, r, value):
        if p >= MSK and r == 16:
            value = value * edge_row
        ext[p, r : r + 8, 256:384] = value

    unpack_columns(recv_e, recv_w, recv_d, PLANES, put_x)

    for lev in range(LEV):
        m = ext[MSK + lev]
        me, mn = m * east(m), m * north(m)
        k, v = ext[DIF + lev] * me, ext[VEL + lev] * me
        coef[EA + lev] = jnp.maximum(v, 0.0) + k
        coef[EB + lev] = jnp.minimum(v, 0.0) - k
        k, v = ext[DIF + LEV + lev] * mn, ext[VEL + LEV + lev] * mn
        coef[NA + lev] = jnp.maximum(v, 0.0) + k
        coef[NB + lev] = jnp.minimum(v, 0.0) - k
        if lev < LEV - 1:
            coef[BK + lev] = ext[DIF + 2 * LEV + lev] * m * ext[MSK + lev + 1]

    def retreat():
        for f in range(2):
            above = None
            for lev in range(LEV):
                p = COT + LEV * f + lev
                v = ext[p]
                step_x, step_y = east(v) - v, north(v) - v
                new = v + (coef[EA + lev] * step_x + west(coef[EB + lev] * step_x))
                new = new + (coef[NA + lev] * step_y + south(coef[NB + lev] * step_y))
                if lev < LEV - 1:
                    vertical = coef[BK + lev] * (ext[p + 1] - v)
                    new = new + vertical
                if above is not None:
                    new = new - above
                above = vertical
                ext[p] = new

    def advance():
        for f in range(2):
            above = None
            for lev in range(LEV):
                p = TRC + LEV * f + lev
                v = ext[p]
                flux_x = coef[EA + lev] * v + coef[EB + lev] * east(v)
                flux_y = coef[NA + lev] * v + coef[NB + lev] * north(v)
                new = v - (flux_x - west(flux_x)) - (flux_y - south(flux_y))
                if lev < LEV - 1:
                    below = coef[BK + lev] * (v - ext[p + 1])
                    new = new - below
                if above is not None:
                    new = new + above
                above = below
                if lev == 0:
                    new = new + force[f]
                ext[p] = new

    for f in range(2):
        ssum[f] = ext[COT + LEV * f, 0:ROWS, 0:COLS]

    @pl.loop(0, STEPS - 1)
    def _(step):
        retreat()
        for f in range(2):
            ssum[f] = ssum[f] + ext[COT + LEV * f, 0:ROWS, 0:COLS]

    mask0 = ext[MSK, 0:ROWS, 0:COLS]
    for f in range(2):
        surface = ssum[f] * mask0
        for h in range(2):
            s_all[lon, pl.ds(2 * h + f, ROWS, stride=4), :] = surface[:, 128 * h : 128 * h + 128]

    ssem = (s_ssem, s_rsem)
    mine = s_all.at[lon]
    row_blocks = s_all.at[pl.ds(4 * plane, 4)]
    near = [remote(mine, mine, ssem, b - 1, in_plane(b)) for b in range(1, 4)]
    far = [remote(row_blocks, row_blocks, ssem, 2 + a, across(a)) for a in range(1, 4)]
    for copy in near:
        copy.start()

    for g in range(16 // 2):
        first, second = (source(BATCH * PLANE_ORDER[2 * g // BATCH] + 2 * g % BATCH + i) for i in range(2))
        pick = jnp.concatenate([ids[pl.ds(first, 1), 0:CAP], ids[pl.ds(second, 1), 0:CAP]], axis=1)
        hot[:, 128 * g : 128 * g + 128] = (pick == iota((ATM, 128), 0)).astype(BF16)

    retreat()
    adjoint_out = pltpu.make_async_copy(ext.at[COT : COT + 8, 0:ROWS, 0:COLS], out_c, out_sem.at[0])
    adjoint_out.start()

    def reverse(batch):
        for i in range(BATCH):
            hi, lo = split(s_all[source(BATCH * PLANE_ORDER[batch] + i)])
            v_cat[MSG * i : MSG * i + MSG, 0:128] = hi
            v_cat[MSG * i : MSG * i + MSG, 128:256] = hi
            v_cat[MSG * (BATCH + i) : MSG * (BATCH + i + 1), 0:128] = lo
            v_cat[MSG * (BATCH + i) : MSG * (BATCH + i + 1), 128:256] = lo
        size = MSG * BATCH

        @pl.loop(0, WB // 2, unroll=8)
        def _(pair):
            both = w_rev[pair]
            out = dot(v_cat[0:size], both) + dot(v_cat[size:], both)
            at = pl.multiple_of(pair * (2 * size), 2 * size)
            table_r[pl.ds(at, size), :] = out[:, 0:128]
            table_r[pl.ds(at + size, size), :] = out[:, 128:256]

        @pl.loop(0, BATCH)
        def _(i):
            k = source(BATCH * PLANE_ORDER[batch] + i)
            base = pl.multiple_of(i * (2 * CAP), 2 * CAP)
            for s in range(CAP):
                at = rows_s[1, k, s] + i * MSG
                z_rows[pl.ds(base + 2 * s, 2), :] = table_r[pl.ds(at, 2), :]

        terms = [split(z_rows[pl.ds(f, BATCH * CAP, stride=2), :]) for f in range(2)]
        rhs = jnp.concatenate([jnp.concatenate([t[i] for t in terms], axis=1) for i in range(2)], axis=0)
        chosen = hot[:, BATCH * CAP * batch : BATCH * CAP * (batch + 1)]
        part = dot(jnp.concatenate([chosen, chosen], axis=1), rhs)
        for f in range(2):
            grad[f] = part[:, 128 * f : 128 * f + 128] + (grad[f] if batch else 0.0)

    for copy in near:
        copy.wait_recv()
    far[0].start()
    far[2].start()

    for copy in partials:
        copy.wait_recv()
    for b in range(4):
        q_send[b] = (p_send[b] + p_recv[4 + b]) + (p_recv[8 + b] + p_recv[12 + b])
    sums = [remote(q_send.at[b], q_recv.at[b], psem, 2 + b, in_plane(b)) for b in range(1, 4)]
    for copy in sums:
        copy.start()
    reverse(0)
    far[1].start()

    total = q_send[0]
    for b in range(1, 4):
        sums[b - 1].wait_recv()
        total = total + q_recv[b]
    q_send[0] = total
    for f in range(2):
        for h in range(2):
            part = q_send[0, pl.ds(2 * h + f, ROWS, stride=4), :]
            force[f, 0:ROWS, 128 * h : 128 * h + 128] = part * mask0[:, 128 * h : 128 * h + 128]
        fsend_r[f] = force[f, 0:ROWS, 0:COLS]

    fsem = (f_send, f_recv)

    def put_f(r, tile, value):
        fsend_c[r : r + 8, :] = value

    pack_columns(lambda p: lambda r, c: force[p, r : r + 8, c : c + 128], 2, put_f)
    fcopies = [
        remote(fsend_r.at[:, 8:16], frecv_s, fsem, 0, (up, lon)),
        remote(fsend_r.at[:, 0:8], frecv_n, fsem, 1, (down, lon)),
    ] + column_copies(fsend_c, frecv_e, frecv_w, frecv_d, fsem, 2)
    for copy in fcopies:
        copy.start()

    for batch in range(1, 4):
        far[PLANE_ORDER[batch] - 1].wait_recv()
        reverse(batch)

    grad_out = pltpu.make_async_copy(grad, out_g, out_sem.at[2])
    grad_out.start()

    for copy in fcopies:
        copy.wait_recv()
    for f in range(2):
        force[f, 16:24, 0:COLS] = jnp.where(low, frecv_n[f], frecv_s[f]) * edge_row2

    def put_force(p, r, value):
        force[p, r : r + 8, 256:384] = value * edge_row if r == 16 else value

    unpack_columns(frecv_e, frecv_w, frecv_d, 2, put_force)

    @pl.loop(0, STEPS)
    def _(step):
        advance()

    tracer_out = pltpu.make_async_copy(ext.at[TRC : TRC + 8, 0:ROWS, 0:COLS], out_t, out_sem.at[1])
    tracer_out.start()

    for copy in halos + fcopies + near + far + partials + sums:
        copy.wait_send()
    adjoint_out.wait()
    tracer_out.wait()
    grad_out.wait()


def place(a, b, c, out_a, out_b, out_c, sem):
    copies = [pltpu.make_async_copy(x, y, sem.at[i]) for i, (x, y) in enumerate(((a, out_a), (b, out_b), (c, out_c)))]
    for copy in copies:
        copy.start()
    for copy in copies:
        copy.wait()


def on_device(n_lat, n_lon, tracers, cotangent, land_mask, diffusion, velocity, weights, atm_state, margins):
    fields = (2 * LEV, ROWS, COLS)
    margins = margins.reshape(3, n_lon, CAP)
    anywhere = pl.BlockSpec(memory_space=pltpu.HBM)

    def buf(*shape, dtype=F32):
        return pltpu.VMEM(shape, dtype)

    dma = pltpu.SemaphoreType.DMA
    scratch = [
        buf(PLANES, XROWS, XCOLS), buf(LEV, ROWS, COLS, dtype=jnp.int32), buf(2, ATM, BLOCK), buf(WB, BLOCK, BLOCK),
        pltpu.SMEM((2, n_lon, 128), jnp.int32), buf(2, n_lon, 128, dtype=jnp.int32), buf(3, n_lon, CAP, dtype=jnp.int32),
        buf(20, XROWS, XCOLS), buf(2, XROWS, XCOLS), buf(2, ROWS, COLS),
        buf(HALF, 8, COLS), buf(HALF, 8, COLS), buf(ROWS, 384), buf(HALF, 8, COLS), buf(HALF, 8, COLS),
        buf(ROWS, 384), buf(ROWS, 384), buf(4, 8, 384),
        buf(2, ROWS, COLS), buf(ROWS, 128), buf(2, 8, COLS), buf(2, 8, COLS),
        buf(ROWS, 128), buf(ROWS, 128), buf(4, 8, 128),
        buf(WB // 2, 256, 256, dtype=BF16), buf(WB // 2, 256, 256, dtype=BF16), buf(2 * ATM, BLOCK),
        buf(4 * ATM, 256, dtype=BF16), buf(WB * 2 * ATM, BLOCK), buf(2 * CAP, BLOCK),
        buf(n_lon, MSG, BLOCK), buf(n_lon, MSG, BLOCK), buf(4, MSG, BLOCK), buf(4, MSG, BLOCK),
        buf(n_lon, MSG, BLOCK), buf(2 * BATCH * MSG, 256, dtype=BF16), buf(WB * BATCH * MSG, BLOCK),
        buf(BATCH * 2 * CAP, BLOCK), buf(16, 128, dtype=jnp.int32),
        buf(ATM, n_lon * CAP, dtype=BF16), buf(n_lon, OCN, 2 * CAP, dtype=BF16), buf(2, ATM, BLOCK),
        dma((9,)), dma((8,)), dma((8,)), dma((6,)), dma((6,)), dma((6,)), dma((6,)), dma((8,)), dma((8,)), dma((3,)),
    ]

    def body(*refs):
        kernel(n_lat, n_lon, *refs)

    out_t, out_c, out_g = pl.pallas_call(
        body,
        out_shape=(
            jax.ShapeDtypeStruct(fields, F32),
            jax.ShapeDtypeStruct(fields, F32),
            jax.ShapeDtypeStruct((2, ATM, BLOCK), F32),
        ),
        in_specs=[anywhere] * 8,
        out_specs=(anywhere, anywhere, anywhere),
        scratch_shapes=scratch,
        compiler_params=pltpu.CompilerParams(collective_id=0, has_side_effects=True, vmem_limit_bytes=48 << 20),
    )(*(pltpu.with_memory_space_constraint(x, pltpu.HBM) for x in (
        tracers.reshape(fields),
        cotangent.reshape(fields),
        land_mask,
        diffusion.reshape(3 * LEV, ROWS, COLS),
        velocity.reshape(fields),
        weights,
        atm_state.reshape(2, ATM, BLOCK),
        margins,
    )))
    out_t, out_c, out_g = pl.pallas_call(
        place,
        out_shape=(
            jax.ShapeDtypeStruct(fields, F32),
            jax.ShapeDtypeStruct(fields, F32),
            jax.ShapeDtypeStruct((2, ATM, BLOCK), F32),
        ),
        in_specs=[pl.BlockSpec(memory_space=pltpu.VMEM)] * 3,
        compiler_params=pltpu.CompilerParams(vmem_limit_bytes=2 << 20),
        out_specs=(anywhere,) * 3,
        scratch_shapes=[dma((3,))],
    )(out_t, out_c, out_g)
    return out_t.reshape(tracers.shape), out_c.reshape(tracers.shape), out_g.reshape(atm_state.shape)


def solution(mesh):
    n_lat, n_lon = mesh.shape["lat"], mesh.shape["lon"]

    def run(*args):
        return on_device(n_lat, n_lon, *args)

    return jax.shard_map(
        run,
        mesh=mesh,
        in_specs=(
            P(None, None, "lat", "lon"),
            P(None, None, "lat", "lon"),
            P(None, "lat", "lon"),
            P(None, None, "lat", "lon"),
            P(None, None, "lat", "lon"),
            P(),
            P(None, "lat", "lon", None),
            P(None, "lat", "lon", None, None),
        ),
        out_specs=(
            P(None, None, "lat", "lon"),
            P(None, None, "lat", "lon"),
            P(None, "lat", "lon", None),
        ),
        check_vma=False,
    )
```

```python
import jax
import jax.numpy as jnp
from jax import lax
from jax.experimental import pallas as pl
from jax.experimental.pallas import tpu as pltpu
from jax.sharding import PartitionSpec as P

MESH = pl.DeviceIdType.MESH
F32 = jnp.float32
BF16 = jnp.bfloat16
BLOCK = 128
CAP = 64
STEPS = 4
LEV = 4
ROWS = 16
COLS = 256
XROWS = 24
XCOLS = 384
TRC, COT, DIF, VEL, MSK = 0, 8, 16, 28, 36
PLANES = 40
HALF = PLANES // 2
EA, EB, NA, NB, BK = 0, 4, 8, 12, 16
WB = 32
ATM = 256
OCN = 32
MSG = 2 * OCN
PLANE_ORDER = (0, 1, 3, 2)
BATCH = 4


def iota(shape, axis):
    return lax.broadcasted_iota(jnp.int32, shape, axis)


def split(x):
    hi = x.astype(BF16)
    return hi, (x - hi.astype(F32)).astype(BF16)


def dot(a, b):
    return lax.dot_general(a, b, (((1,), (0,)), ((), ())), preferred_element_type=F32)


def dot_t(a, b):
    return lax.dot_general(a, b, (((1,), (1,)), ((), ())), preferred_element_type=F32)


def east(x):
    return pltpu.roll(x, XCOLS - 1, 1)


def west(x):
    return pltpu.roll(x, 1, 1)


def north(x):
    return pltpu.roll(x, XROWS - 1, 0)


def south(x):
    return pltpu.roll(x, 1, 0)


def kernel(
    n_lat, n_lon,
    tracers, cotangent, land, diffusion, velocity, weights, atm, margins,
    out_t, out_c, out_g,
    ext, mask_i, atm_v, weights_v, rows_s, rows_v, slots_v, coef, force, ssum,
    send_n, send_s, send_c, recv_n, recv_s, recv_e, recv_w, recv_d,
    fsend_r, fsend_c, frecv_n, frecv_s, frecv_e, frecv_w, frecv_d,
    w_fwd, w_rev, x_rows, x_cat, table_f, picked, p_send, p_recv, q_send, q_recv,
    s_all, v_cat, table_r, z_rows, ids, hot, hot_o, grad,
    load_sem, halo_send, halo_recv, p_ssem, p_rsem, s_ssem, s_rsem, f_send, f_recv, out_sem,
):
    lat, lon = lax.axis_index("lat"), lax.axis_index("lon")
    up, down = lax.rem(lat + 1, n_lat), lax.rem(lat + n_lat - 1, n_lat)
    right, left = lax.rem(lon + 1, n_lon), lax.rem(lon + n_lon - 1, n_lon)
    loads = [
        (tracers, ext.at[TRC : TRC + 8, 0:ROWS, 0:COLS]),
        (cotangent, ext.at[COT : COT + 8, 0:ROWS, 0:COLS]),
        (diffusion, ext.at[DIF : DIF + 12, 0:ROWS, 0:COLS]),
        (velocity, ext.at[VEL : VEL + 8, 0:ROWS, 0:COLS]),
        (land, mask_i),
        (margins, slots_v),
        (atm, atm_v),
        (weights, weights_v),
    ]
    loads = [pltpu.make_async_copy(a, b, load_sem.at[i]) for i, (a, b) in enumerate(loads)]
    for copy in loads[:7]:
        copy.start()

    barrier = pltpu.get_barrier_semaphore()
    plane, place = lax.div(lon, 4), lax.rem(lon, 4)

    def in_plane(b):
        return (lat, 4 * plane + lax.rem(place + b, 4))

    def across(a):
        return (lat, 4 * lax.rem(plane + a, 4) + place)

    peers = [(up, lon), (down, lon), (up, left), (up, right), (down, left), (down, right), (lat, left), (lat, right)]
    peers += [in_plane(i) for i in range(1, 4)] + [across(i) for i in range(1, 4)]
    for peer in peers:
        pl.semaphore_signal(barrier, inc=1, device_id=peer, device_id_type=MESH)


    def target(step):
        return 4 * lax.rem(plane + lax.div(step, 4), 4) + lax.rem(place + lax.rem(step, 4), 4)

    def source(step):
        return 4 * lax.rem(plane + 4 - lax.div(step, 4), 4) + lax.rem(place + 4 - lax.rem(step, 4), 4)

    lane = iota((8, 128), 1)
    row = iota((8, 128), 0)
    row2 = iota((8, COLS), 0)
    low = row2 < 4
    group = lax.rem((lane + 4) // 8, 16)
    for copy in loads[:6]:
        copy.wait()
    loads[7].start()
    ext[MSK : MSK + 4, 0:ROWS, 0:COLS] = mask_i[...].astype(F32)

    @pl.loop(0, HALF)
    def _(p):
        first, last = ext[p, 0:8, 0:COLS], ext[p, 8:16, 0:COLS]
        first2, last2 = ext[p + HALF, 0:8, 0:COLS], ext[p + HALF, 8:16, 0:COLS]
        send_n[p] = jnp.where(low, pltpu.roll(last2, 4, 0), last)
        send_s[p] = jnp.where(low, first, pltpu.roll(first2, 4, 0))

    def remote(src, dst, sems, i, peer):
        return pltpu.make_async_remote_copy(
            src_ref=src, dst_ref=dst, send_sem=sems[0].at[i], recv_sem=sems[1].at[i], device_id=peer, device_id_type=MESH
        )

    ids[:, 0:CAP] = jnp.where(slots_v[0] >= 0, slots_v[1], -1)
    rows_v[0, :, 0:CAP] = slots_v[2] * (2 * ATM) + 2 * slots_v[1]
    rows_v[1, :, 0:CAP] = slots_v[2] * (MSG * BATCH) + 2 * jnp.maximum(slots_v[0], 0)
    index_copy = pltpu.make_async_copy(rows_v, rows_s, load_sem.at[8])
    index_copy.start()

    def pack_columns(plane_of, count, put):
        for tile in range(-(-count // 16)):
            for r in (0, 8):
                acc = jnp.zeros((8, 128), F32)
                for q in range(min(16, count - 16 * tile)):
                    p = plane_of(16 * tile + q)
                    edge = jnp.where(lane < 4, p(r, 0), p(r, 128))
                    if q:
                        edge = pltpu.roll(edge, 8 * q, 1)
                    acc = jnp.where(group == q, edge, acc)
                put(r, tile, acc)

    def put_c(r, tile, value):
        send_c[r : r + 8, 128 * tile : 128 * tile + 128] = value

    pack_columns(lambda p: lambda r, c: ext[p, r : r + 8, c : c + 128], PLANES, put_c)

    def column_copies(src, to_e, to_w, to_d, sems, base):
        first, last = src.at[0:8], src.at[8:16]
        return [
            remote(src, to_w, sems, base, (lat, right)),
            remote(src, to_e, sems, base + 1, (lat, left)),
            remote(last, to_d.at[3], sems, base + 2, (up, right)),
            remote(last, to_d.at[1], sems, base + 3, (up, left)),
            remote(first, to_d.at[2], sems, base + 4, (down, right)),
            remote(first, to_d.at[0], sems, base + 5, (down, left)),
        ]


    @pl.loop(0, n_lon, unroll=4)
    def _(step):
        k = target(step)
        onehot = (slots_v[0, pl.ds(k, 1), :] == iota((OCN, CAP), 0)).astype(BF16)
        hot_o[step, :, 0:CAP] = onehot
        hot_o[step, :, CAP:] = onehot

    pl.semaphore_wait(barrier, len(peers))

    halo = (halo_send, halo_recv)
    halos = [remote(send_n, recv_s, halo, 0, (up, lon)), remote(send_s, recv_n, halo, 1, (down, lon))]
    for copy in halos:
        copy.start()

    columns = column_copies(send_c, recv_e, recv_w, recv_d, halo, 2)
    for copy in columns:
        copy.start()
    halos += columns

    for copy in loads[6:]:
        copy.wait()
    index_copy.wait()

    @pl.loop(0, WB // 2)
    def _(pair):
        for i in range(2):
            hi, lo = split(weights_v[2 * pair + i])
            w_fwd[pair, 128 * i : 128 * i + 128, 0:128] = hi
            w_fwd[pair, 128 * i : 128 * i + 128, 128:256] = lo
            w_rev[pair, 0:128, 128 * i : 128 * i + 128] = hi
            w_rev[pair, 128:256, 128 * i : 128 * i + 128] = lo

    for f in range(2):
        x_rows[pl.ds(f, ATM, stride=2), :] = atm_v[f]
    hi, lo = split(x_rows[...])
    x_cat[0 : 2 * ATM, 0:128] = hi
    x_cat[0 : 2 * ATM, 128:256] = hi
    x_cat[2 * ATM :, 0:128] = lo
    x_cat[2 * ATM :, 128:256] = lo

    @pl.loop(0, WB // 2, unroll=8)
    def _(pair):
        both = w_fwd[pair]
        out = dot_t(x_cat[0 : 2 * ATM], both) + dot_t(x_cat[2 * ATM :], both)
        at = pl.multiple_of(pair * (4 * ATM), 4 * ATM)
        table_f[pl.ds(at, 2 * ATM), :] = out[:, 0:128]
        table_f[pl.ds(at + 2 * ATM, 2 * ATM), :] = out[:, 128:256]

    def partial(step):
        k = target(step)
        for s in range(CAP):
            at = rows_s[0, k, s]
            picked[2 * s : 2 * s + 2, :] = table_f[pl.ds(at, 2), :]
        terms = [split(picked[pl.ds(f, CAP, stride=2), :]) for f in range(2)]
        rhs = jnp.concatenate([jnp.concatenate([t[i] for t in terms], axis=1) for i in range(2)], axis=0)
        sums = dot(hot_o[step], rhs)
        for f in range(2):
            p_send[step, pl.ds(f, OCN, stride=2), :] = sums[:, 128 * f : 128 * f + 128]

    psem = (p_ssem, p_rsem)

    partials = [remote(p_send.at[4 * a : 4 * a + 4], p_recv.at[4 * a : 4 * a + 4], psem, a - 1, across(a)) for a in range(1, 4)]
    for a in (1, 3, 2):
        pl.loop(4 * a, 4 * a + 4, unroll=4)(partial)
        partials[a - 1].start()

    for copy in halos:
        copy.wait_recv()

    edge_row = jnp.where(row < 4, (lat < n_lat - 1).astype(F32), (lat > 0).astype(F32))
    edge_row2 = jnp.where(low, (lat < n_lat - 1).astype(F32), (lat > 0).astype(F32))

    @pl.loop(0, HALF)
    def _(p):
        from_n, from_s = recv_n[p], recv_s[p]
        ext[p, 16:24, 0:COLS] = jnp.where(low, from_n, from_s)
        ext[p + HALF, 16:24, 0:COLS] = pltpu.roll(jnp.where(low, from_s, from_n), 4, 0)

    for p in range(MSK, MSK + 4):
        ext[p, 16:24, 0:COLS] = ext[p, 16:24, 0:COLS] * edge_row2

    from_east = lax.rem(lane, 8) < 4
    keep = jnp.logical_or(lane < 4, lane >= 124)

    def unpack_columns(from_e, from_w, from_d, count, put):
        for tile in range(-(-count // 16)):
            t = slice(128 * tile, 128 * tile + 128)
            for r in (0, 8, 16):
                if r < 16:
                    e, w = from_e[r : r + 8, t], from_w[r : r + 8, t]
                else:
                    e = jnp.where(row < 4, from_d[0, :, t], from_d[1, :, t])
                    w = jnp.where(row < 4, from_d[2, :, t], from_d[3, :, t])
                both = jnp.where(from_east, e, w)
                for q in range(min(16, count - 16 * tile)):
                    value = pltpu.roll(both, 128 - 8 * q, 1) if q else both
                    put(16 * tile + q, r, jnp.where(keep, value, 0.0))

    def put_x(p, r, value):
        if p >= MSK and r == 16:
            value = value * edge_row
        ext[p, r : r + 8, 256:384] = value

    unpack_columns(recv_e, recv_w, recv_d, PLANES, put_x)

    for lev in range(LEV):
        m = ext[MSK + lev]
        me, mn = m * east(m), m * north(m)
        k, v = ext[DIF + lev] * me, ext[VEL + lev] * me
        coef[EA + lev] = jnp.maximum(v, 0.0) + k
        coef[EB + lev] = jnp.minimum(v, 0.0) - k
        k, v = ext[DIF + LEV + lev] * mn, ext[VEL + LEV + lev] * mn
        coef[NA + lev] = jnp.maximum(v, 0.0) + k
        coef[NB + lev] = jnp.minimum(v, 0.0) - k
        if lev < LEV - 1:
            coef[BK + lev] = ext[DIF + 2 * LEV + lev] * m * ext[MSK + lev + 1]

    def retreat():
        for f in range(2):
            above = None
            for lev in range(LEV):
                p = COT + LEV * f + lev
                v = ext[p]
                step_x, step_y = east(v) - v, north(v) - v
                new = v + (coef[EA + lev] * step_x + west(coef[EB + lev] * step_x))
                new = new + (coef[NA + lev] * step_y + south(coef[NB + lev] * step_y))
                if lev < LEV - 1:
                    vertical = coef[BK + lev] * (ext[p + 1] - v)
                    new = new + vertical
                if above is not None:
                    new = new - above
                above = vertical
                ext[p] = new

    def advance():
        for f in range(2):
            above = None
            for lev in range(LEV):
                p = TRC + LEV * f + lev
                v = ext[p]
                flux_x = coef[EA + lev] * v + coef[EB + lev] * east(v)
                flux_y = coef[NA + lev] * v + coef[NB + lev] * north(v)
                new = v - (flux_x - west(flux_x)) - (flux_y - south(flux_y))
                if lev < LEV - 1:
                    below = coef[BK + lev] * (v - ext[p + 1])
                    new = new - below
                if above is not None:
                    new = new + above
                above = below
                if lev == 0:
                    new = new + force[f]
                ext[p] = new

    for f in range(2):
        ssum[f] = ext[COT + LEV * f, 0:ROWS, 0:COLS]

    @pl.loop(0, STEPS - 1)
    def _(step):
        retreat()
        for f in range(2):
            ssum[f] = ssum[f] + ext[COT + LEV * f, 0:ROWS, 0:COLS]

    mask0 = ext[MSK, 0:ROWS, 0:COLS]
    for f in range(2):
        surface = ssum[f] * mask0
        for h in range(2):
            s_all[lon, pl.ds(2 * h + f, ROWS, stride=4), :] = surface[:, 128 * h : 128 * h + 128]

    ssem = (s_ssem, s_rsem)
    mine = s_all.at[lon]
    row_blocks = s_all.at[pl.ds(4 * plane, 4)]
    near = [remote(mine, mine, ssem, b - 1, in_plane(b)) for b in range(1, 4)]
    far = [remote(row_blocks, row_blocks, ssem, 2 + a, across(a)) for a in range(1, 4)]
    for copy in near:
        copy.start()

    pl.loop(0, 4, unroll=4)(partial)

    for g in range(16 // 2):
        first, second = (source(BATCH * PLANE_ORDER[2 * g // BATCH] + 2 * g % BATCH + i) for i in range(2))
        pick = jnp.concatenate([ids[pl.ds(first, 1), 0:CAP], ids[pl.ds(second, 1), 0:CAP]], axis=1)
        hot[:, 128 * g : 128 * g + 128] = (pick == iota((ATM, 128), 0)).astype(BF16)

    retreat()
    adjoint_out = pltpu.make_async_copy(ext.at[COT : COT + 8, 0:ROWS, 0:COLS], out_c, out_sem.at[0])
    adjoint_out.start()

    def gather(batch):
        count = BATCH * CAP
        terms = [split(z_rows[pl.ds(2 * count * batch + f, count, stride=2), :]) for f in range(2)]
        rhs = jnp.concatenate([jnp.concatenate([t[i] for t in terms], axis=1) for i in range(2)], axis=0)
        chosen = hot[:, count * batch : count * (batch + 1)]
        part = dot(jnp.concatenate([chosen, chosen], axis=1), rhs)
        for f in range(2):
            grad[f] = part[:, 128 * f : 128 * f + 128] + (grad[f] if batch else 0.0)

    def reverse(batch):
        for i in range(BATCH):
            hi, lo = split(s_all[source(BATCH * PLANE_ORDER[batch] + i)])
            v_cat[MSG * i : MSG * i + MSG, 0:128] = hi
            v_cat[MSG * i : MSG * i + MSG, 128:256] = hi
            v_cat[MSG * (BATCH + i) : MSG * (BATCH + i + 1), 0:128] = lo
            v_cat[MSG * (BATCH + i) : MSG * (BATCH + i + 1), 128:256] = lo
        size = MSG * BATCH

        @pl.loop(0, WB // 2, unroll=16)
        def _(pair):
            both = w_rev[pair]
            out = dot(v_cat[0:size], both) + dot(v_cat[size:], both)
            at = pl.multiple_of(pair * (2 * size), 2 * size)
            table_r[pl.ds(at, size), :] = out[:, 0:128]
            table_r[pl.ds(at + size, size), :] = out[:, 128:256]

        if batch:
            gather(batch - 1)

        @pl.loop(0, BATCH, unroll=4)
        def _(i):
            k = source(BATCH * PLANE_ORDER[batch] + i)
            base = pl.multiple_of((batch * BATCH + i) * (2 * CAP), 2 * CAP)
            for s in range(CAP):
                at = rows_s[1, k, s] + i * MSG
                z_rows[pl.ds(base + 2 * s, 2), :] = table_r[pl.ds(at, 2), :]

    for copy in near:
        copy.wait_recv()
    far[0].start()
    far[2].start()

    for copy in partials:
        copy.wait_recv()
    for b in range(4):
        q_send[b] = (p_send[b] + p_recv[4 + b]) + (p_recv[8 + b] + p_recv[12 + b])
    sums = [remote(q_send.at[b], q_recv.at[b], psem, 2 + b, in_plane(b)) for b in range(1, 4)]
    for copy in sums:
        copy.start()
    reverse(0)
    far[1].start()
    total = q_send[0]
    for b in range(1, 4):
        sums[b - 1].wait_recv()
        total = total + q_recv[b]
    q_send[0] = total
    for f in range(2):
        for h in range(2):
            part = q_send[0, pl.ds(2 * h + f, ROWS, stride=4), :]
            force[f, 0:ROWS, 128 * h : 128 * h + 128] = part * mask0[:, 128 * h : 128 * h + 128]
        fsend_r[f] = force[f, 0:ROWS, 0:COLS]

    fsem = (f_send, f_recv)

    def put_f(r, tile, value):
        fsend_c[r : r + 8, :] = value

    pack_columns(lambda p: lambda r, c: force[p, r : r + 8, c : c + 128], 2, put_f)
    fcopies = [
        remote(fsend_r.at[:, 8:16], frecv_s, fsem, 0, (up, lon)),
        remote(fsend_r.at[:, 0:8], frecv_n, fsem, 1, (down, lon)),
    ] + column_copies(fsend_c, frecv_e, frecv_w, frecv_d, fsem, 2)
    for copy in fcopies:
        copy.start()

    far[PLANE_ORDER[1] - 1].wait_recv()
    reverse(1)
    far[PLANE_ORDER[2] - 1].wait_recv()
    reverse(2)
    far[PLANE_ORDER[3] - 1].wait_recv()
    reverse(3)

    gather(3)
    grad_out = pltpu.make_async_copy(grad, out_g, out_sem.at[2])
    grad_out.start()

    for copy in fcopies:
        copy.wait_recv()
    for f in range(2):
        force[f, 16:24, 0:COLS] = jnp.where(low, frecv_n[f], frecv_s[f]) * edge_row2

    def put_force(p, r, value):
        force[p, r : r + 8, 256:384] = value * edge_row if r == 16 else value

    unpack_columns(frecv_e, frecv_w, frecv_d, 2, put_force)

    @pl.loop(0, STEPS)
    def _(step):
        advance()

    tracer_out = pltpu.make_async_copy(ext.at[TRC : TRC + 8, 0:ROWS, 0:COLS], out_t, out_sem.at[1])
    tracer_out.start()

    for copy in halos + fcopies + near + far + partials + sums:
        copy.wait_send()
    adjoint_out.wait()
    tracer_out.wait()
    grad_out.wait()


def place(a, b, c, out_a, out_b, out_c, sem):
    copies = [pltpu.make_async_copy(x, y, sem.at[i]) for i, (x, y) in enumerate(((a, out_a), (b, out_b), (c, out_c)))]
    for copy in copies:
        copy.start()
    for copy in copies:
        copy.wait()


def on_device(n_lat, n_lon, tracers, cotangent, land_mask, diffusion, velocity, weights, atm_state, margins):
    fields = (2 * LEV, ROWS, COLS)
    margins = margins.reshape(3, n_lon, CAP)
    anywhere = pl.BlockSpec(memory_space=pltpu.HBM)

    def buf(*shape, dtype=F32):
        return pltpu.VMEM(shape, dtype)

    dma = pltpu.SemaphoreType.DMA
    scratch = [
        buf(PLANES, XROWS, XCOLS), buf(LEV, ROWS, COLS, dtype=jnp.int32), buf(2, ATM, BLOCK), buf(WB, BLOCK, BLOCK),
        pltpu.SMEM((2, n_lon, 128), jnp.int32), buf(2, n_lon, 128, dtype=jnp.int32), buf(3, n_lon, CAP, dtype=jnp.int32),
        buf(20, XROWS, XCOLS), buf(2, XROWS, XCOLS), buf(2, ROWS, COLS),
        buf(HALF, 8, COLS), buf(HALF, 8, COLS), buf(ROWS, 384), buf(HALF, 8, COLS), buf(HALF, 8, COLS),
        buf(ROWS, 384), buf(ROWS, 384), buf(4, 8, 384),
        buf(2, ROWS, COLS), buf(ROWS, 128), buf(2, 8, COLS), buf(2, 8, COLS),
        buf(ROWS, 128), buf(ROWS, 128), buf(4, 8, 128),
        buf(WB // 2, 256, 256, dtype=BF16), buf(WB // 2, 256, 256, dtype=BF16), buf(2 * ATM, BLOCK),
        buf(4 * ATM, 256, dtype=BF16), buf(WB * 2 * ATM, BLOCK), buf(2 * CAP, BLOCK),
        buf(n_lon, MSG, BLOCK), buf(n_lon, MSG, BLOCK), buf(4, MSG, BLOCK), buf(4, MSG, BLOCK),
        buf(n_lon, MSG, BLOCK), buf(2 * BATCH * MSG, 256, dtype=BF16), buf(WB * BATCH * MSG, BLOCK),
        buf(n_lon * 2 * CAP, BLOCK), buf(16, 128, dtype=jnp.int32),
        buf(ATM, n_lon * CAP, dtype=BF16), buf(n_lon, OCN, 2 * CAP, dtype=BF16), buf(2, ATM, BLOCK),
        dma((9,)), dma((8,)), dma((8,)), dma((6,)), dma((6,)), dma((6,)), dma((6,)), dma((8,)), dma((8,)), dma((3,)),
    ]

    def body(*refs):
        kernel(n_lat, n_lon, *refs)

    out_t, out_c, out_g = pl.pallas_call(
        body,
        out_shape=(
            jax.ShapeDtypeStruct(fields, F32),
            jax.ShapeDtypeStruct(fields, F32),
            jax.ShapeDtypeStruct((2, ATM, BLOCK), F32),
        ),
        in_specs=[anywhere] * 8,
        out_specs=(anywhere, anywhere, anywhere),
        scratch_shapes=scratch,
        compiler_params=pltpu.CompilerParams(collective_id=0, has_side_effects=True, vmem_limit_bytes=48 << 20),
    )(*(pltpu.with_memory_space_constraint(x, pltpu.HBM) for x in (
        tracers.reshape(fields),
        cotangent.reshape(fields),
        land_mask,
        diffusion.reshape(3 * LEV, ROWS, COLS),
        velocity.reshape(fields),
        weights,
        atm_state.reshape(2, ATM, BLOCK),
        margins,
    )))
    out_t, out_c, out_g = pl.pallas_call(
        place,
        out_shape=(
            jax.ShapeDtypeStruct(fields, F32),
            jax.ShapeDtypeStruct(fields, F32),
            jax.ShapeDtypeStruct((2, ATM, BLOCK), F32),
        ),
        in_specs=[pl.BlockSpec(memory_space=pltpu.VMEM)] * 3,
        compiler_params=pltpu.CompilerParams(vmem_limit_bytes=2 << 20),
        out_specs=(anywhere,) * 3,
        scratch_shapes=[dma((3,))],
    )(out_t, out_c, out_g)
    return out_t.reshape(tracers.shape), out_c.reshape(tracers.shape), out_g.reshape(atm_state.shape)


def solution(mesh):
    n_lat, n_lon = mesh.shape["lat"], mesh.shape["lon"]

    def run(*args):
        return on_device(n_lat, n_lon, *args)

    return jax.shard_map(
        run,
        mesh=mesh,
        in_specs=(
            P(None, None, "lat", "lon"),
            P(None, None, "lat", "lon"),
            P(None, "lat", "lon"),
            P(None, None, "lat", "lon"),
            P(None, None, "lat", "lon"),
            P(),
            P(None, "lat", "lon", None),
            P(None, "lat", "lon", None, None),
        ),
        out_specs=(
            P(None, None, "lat", "lon"),
            P(None, None, "lat", "lon"),
            P(None, "lat", "lon", None),
        ),
        check_vma=False,
    )
```

```python
import jax
import jax.numpy as jnp
from jax import lax
from jax.experimental import pallas as pl
from jax.experimental.pallas import tpu as pltpu
from jax.sharding import PartitionSpec as P

MESH = pl.DeviceIdType.MESH
F32 = jnp.float32
BF16 = jnp.bfloat16
BLOCK = 128
CAP = 64
STEPS = 4
LEV = 4
ROWS = 16
COLS = 256
XROWS = 24
XCOLS = 384
TRC, COT, DIF, VEL, MSK = 0, 8, 16, 28, 36
PLANES = 40
HALF = PLANES // 2
EA, EB, NA, NB, BK = 0, 4, 8, 12, 16
WB = 32
ATM = 256
OCN = 32
MSG = 2 * OCN
PLANE_ORDER = (0, 1, 3, 2)
BATCH = 4


def iota(shape, axis):
    return lax.broadcasted_iota(jnp.int32, shape, axis)


def split(x):
    hi = x.astype(BF16)
    return hi, (x - hi.astype(F32)).astype(BF16)


def dot(a, b):
    return lax.dot_general(a, b, (((1,), (0,)), ((), ())), preferred_element_type=F32)


def dot_t(a, b):
    return lax.dot_general(a, b, (((1,), (1,)), ((), ())), preferred_element_type=F32)


def east(x):
    return pltpu.roll(x, XCOLS - 1, 1)


def west(x):
    return pltpu.roll(x, 1, 1)


def north(x):
    return pltpu.roll(x, XROWS - 1, 0)


def south(x):
    return pltpu.roll(x, 1, 0)


def kernel(
    n_lat, n_lon,
    tracers, cotangent, land, diffusion, velocity, weights, atm, margins,
    out_t, out_c, out_g,
    ext, mask_i, atm_v, weights_v, rows_s, rows_v, slots_v, coef, force, ssum,
    send_n, send_s, send_c, recv_n, recv_s, recv_e, recv_w, recv_d,
    fsend_r, fsend_c, frecv_n, frecv_s, frecv_e, frecv_w, frecv_d,
    w_fwd, w_rev, x_rows, x_cat, table_f, picked, p_send, p_recv, q_send, q_recv,
    s_all, v_cat, table_r, z_rows, ids, hot, hot_o, grad,
    load_sem, halo_send, halo_recv, p_ssem, p_rsem, s_ssem, s_rsem, f_send, f_recv, out_sem,
):
    lat, lon = lax.axis_index("lat"), lax.axis_index("lon")
    up, down = lax.rem(lat + 1, n_lat), lax.rem(lat + n_lat - 1, n_lat)
    right, left = lax.rem(lon + 1, n_lon), lax.rem(lon + n_lon - 1, n_lon)
    loads = [
        (tracers, ext.at[TRC : TRC + 8, 0:ROWS, 0:COLS]),
        (cotangent, ext.at[COT : COT + 8, 0:ROWS, 0:COLS]),
        (diffusion, ext.at[DIF : DIF + 12, 0:ROWS, 0:COLS]),
        (velocity, ext.at[VEL : VEL + 8, 0:ROWS, 0:COLS]),
        (land, mask_i),
        (margins, slots_v),
        (atm, atm_v),
        (weights, weights_v),
    ]
    loads = [pltpu.make_async_copy(a, b, load_sem.at[i]) for i, (a, b) in enumerate(loads)]
    for copy in loads[:7]:
        copy.start()

    barrier = pltpu.get_barrier_semaphore()
    plane, place = lax.div(lon, 4), lax.rem(lon, 4)

    def in_plane(b):
        return (lat, 4 * plane + lax.rem(place + b, 4))

    def across(a):
        return (lat, 4 * lax.rem(plane + a, 4) + place)

    peers = [(up, lon), (down, lon), (up, left), (up, right), (down, left), (down, right), (lat, left), (lat, right)]
    peers += [in_plane(i) for i in range(1, 4)] + [across(i) for i in range(1, 4)]
    for peer in peers:
        pl.semaphore_signal(barrier, inc=1, device_id=peer, device_id_type=MESH)


    def target(step):
        return 4 * lax.rem(plane + lax.div(step, 4), 4) + lax.rem(place + lax.rem(step, 4), 4)

    def source(step):
        return 4 * lax.rem(plane + 4 - lax.div(step, 4), 4) + lax.rem(place + 4 - lax.rem(step, 4), 4)

    lane = iota((8, 128), 1)
    row = iota((8, 128), 0)
    row2 = iota((8, COLS), 0)
    low = row2 < 4
    group = lax.rem((lane + 4) // 8, 16)
    for copy in loads[:6]:
        copy.wait()
    loads[7].start()
    ext[MSK : MSK + 4, 0:ROWS, 0:COLS] = mask_i[...].astype(F32)

    @pl.loop(0, HALF)
    def _(p):
        first, last = ext[p, 0:8, 0:COLS], ext[p, 8:16, 0:COLS]
        first2, last2 = ext[p + HALF, 0:8, 0:COLS], ext[p + HALF, 8:16, 0:COLS]
        send_n[p] = jnp.where(low, pltpu.roll(last2, 4, 0), last)
        send_s[p] = jnp.where(low, first, pltpu.roll(first2, 4, 0))

    def remote(src, dst, sems, i, peer):
        return pltpu.make_async_remote_copy(
            src_ref=src, dst_ref=dst, send_sem=sems[0].at[i], recv_sem=sems[1].at[i], device_id=peer, device_id_type=MESH
        )

    ids[:, 0:CAP] = jnp.where(slots_v[0] >= 0, slots_v[1], -1)
    rows_v[0, :, 0:CAP] = slots_v[2] * (2 * ATM) + 2 * slots_v[1]
    rows_v[1, :, 0:CAP] = slots_v[2] * (MSG * BATCH) + 2 * jnp.maximum(slots_v[0], 0)
    index_copy = pltpu.make_async_copy(rows_v, rows_s, load_sem.at[8])
    index_copy.start()

    def pack_columns(plane_of, count, put):
        for tile in range(-(-count // 16)):
            for r in (0, 8):
                acc = jnp.zeros((8, 128), F32)
                for q in range(min(16, count - 16 * tile)):
                    p = plane_of(16 * tile + q)
                    edge = jnp.where(lane < 4, p(r, 0), p(r, 128))
                    if q:
                        edge = pltpu.roll(edge, 8 * q, 1)
                    acc = jnp.where(group == q, edge, acc)
                put(r, tile, acc)

    def put_c(r, tile, value):
        send_c[r : r + 8, 128 * tile : 128 * tile + 128] = value

    pack_columns(lambda p: lambda r, c: ext[p, r : r + 8, c : c + 128], PLANES, put_c)

    def column_copies(src, to_e, to_w, to_d, sems, base):
        first, last = src.at[0:8], src.at[8:16]
        return [
            remote(src, to_w, sems, base, (lat, right)),
            remote(src, to_e, sems, base + 1, (lat, left)),
            remote(last, to_d.at[3], sems, base + 2, (up, right)),
            remote(last, to_d.at[1], sems, base + 3, (up, left)),
            remote(first, to_d.at[2], sems, base + 4, (down, right)),
            remote(first, to_d.at[0], sems, base + 5, (down, left)),
        ]


    @pl.loop(0, n_lon, unroll=4)
    def _(step):
        k = target(step)
        onehot = (slots_v[0, pl.ds(k, 1), :] == iota((OCN, CAP), 0)).astype(BF16)
        hot_o[step, :, 0:CAP] = onehot
        hot_o[step, :, CAP:] = onehot

    pl.semaphore_wait(barrier, len(peers))

    halo = (halo_send, halo_recv)
    halos = [remote(send_n, recv_s, halo, 0, (up, lon)), remote(send_s, recv_n, halo, 1, (down, lon))]
    for copy in halos:
        copy.start()

    columns = column_copies(send_c, recv_e, recv_w, recv_d, halo, 2)
    for copy in columns:
        copy.start()
    halos += columns

    for copy in loads[6:]:
        copy.wait()
    index_copy.wait()

    @pl.loop(0, WB // 2)
    def _(pair):
        for i in range(2):
            hi, lo = split(weights_v[2 * pair + i])
            w_fwd[pair, 128 * i : 128 * i + 128, 0:128] = hi
            w_fwd[pair, 128 * i : 128 * i + 128, 128:256] = lo
            w_rev[pair, 0:128, 128 * i : 128 * i + 128] = hi
            w_rev[pair, 128:256, 128 * i : 128 * i + 128] = lo

    for f in range(2):
        x_rows[pl.ds(f, ATM, stride=2), :] = atm_v[f]
    hi, lo = split(x_rows[...])
    x_cat[0 : 2 * ATM, 0:128] = hi
    x_cat[0 : 2 * ATM, 128:256] = hi
    x_cat[2 * ATM :, 0:128] = lo
    x_cat[2 * ATM :, 128:256] = lo

    @pl.loop(0, WB // 2, unroll=8)
    def _(pair):
        both = w_fwd[pair]
        out = dot_t(x_cat[0 : 2 * ATM], both) + dot_t(x_cat[2 * ATM :], both)
        at = pl.multiple_of(pair * (4 * ATM), 4 * ATM)
        table_f[pl.ds(at, 2 * ATM), :] = out[:, 0:128]
        table_f[pl.ds(at + 2 * ATM, 2 * ATM), :] = out[:, 128:256]

    def partial(step):
        k = target(step)
        for s in range(CAP):
            at = rows_s[0, k, s]
            picked[2 * s : 2 * s + 2, :] = table_f[pl.ds(at, 2), :]
        terms = [split(picked[pl.ds(f, CAP, stride=2), :]) for f in range(2)]
        rhs = jnp.concatenate([jnp.concatenate([t[i] for t in terms], axis=1) for i in range(2)], axis=0)
        sums = dot(hot_o[step], rhs)
        for f in range(2):
            p_send[step, pl.ds(f, OCN, stride=2), :] = sums[:, 128 * f : 128 * f + 128]

    psem = (p_ssem, p_rsem)

    partials = [remote(p_send.at[4 * a : 4 * a + 4], p_recv.at[4 * a : 4 * a + 4], psem, a - 1, across(a)) for a in range(1, 4)]
    for a in (1, 3, 2):
        pl.loop(4 * a, 4 * a + 4, unroll=4)(partial)
        partials[a - 1].start()

    for copy in halos:
        copy.wait_recv()

    edge_row = jnp.where(row < 4, (lat < n_lat - 1).astype(F32), (lat > 0).astype(F32))
    edge_row2 = jnp.where(low, (lat < n_lat - 1).astype(F32), (lat > 0).astype(F32))

    @pl.loop(0, HALF)
    def _(p):
        from_n, from_s = recv_n[p], recv_s[p]
        ext[p, 16:24, 0:COLS] = jnp.where(low, from_n, from_s)
        ext[p + HALF, 16:24, 0:COLS] = pltpu.roll(jnp.where(low, from_s, from_n), 4, 0)

    for p in range(MSK, MSK + 4):
        ext[p, 16:24, 0:COLS] = ext[p, 16:24, 0:COLS] * edge_row2

    from_east = lax.rem(lane, 8) < 4
    keep = jnp.logical_or(lane < 4, lane >= 124)

    def unpack_columns(from_e, from_w, from_d, count, put):
        for tile in range(-(-count // 16)):
            t = slice(128 * tile, 128 * tile + 128)
            for r in (0, 8, 16):
                if r < 16:
                    e, w = from_e[r : r + 8, t], from_w[r : r + 8, t]
                else:
                    e = jnp.where(row < 4, from_d[0, :, t], from_d[1, :, t])
                    w = jnp.where(row < 4, from_d[2, :, t], from_d[3, :, t])
                both = jnp.where(from_east, e, w)
                for q in range(min(16, count - 16 * tile)):
                    value = pltpu.roll(both, 128 - 8 * q, 1) if q else both
                    put(16 * tile + q, r, jnp.where(keep, value, 0.0))

    def put_x(p, r, value):
        if p >= MSK and r == 16:
            value = value * edge_row
        ext[p, r : r + 8, 256:384] = value

    unpack_columns(recv_e, recv_w, recv_d, PLANES, put_x)

    for lev in range(LEV):
        m = ext[MSK + lev]
        me, mn = m * east(m), m * north(m)
        k, v = ext[DIF + lev] * me, ext[VEL + lev] * me
        coef[EA + lev] = jnp.maximum(v, 0.0) + k
        coef[EB + lev] = jnp.minimum(v, 0.0) - k
        k, v = ext[DIF + LEV + lev] * mn, ext[VEL + LEV + lev] * mn
        coef[NA + lev] = jnp.maximum(v, 0.0) + k
        coef[NB + lev] = jnp.minimum(v, 0.0) - k
        if lev < LEV - 1:
            coef[BK + lev] = ext[DIF + 2 * LEV + lev] * m * ext[MSK + lev + 1]

    def retreat():
        for f in range(2):
            above = None
            for lev in range(LEV):
                p = COT + LEV * f + lev
                v = ext[p]
                step_x, step_y = east(v) - v, north(v) - v
                new = v + (coef[EA + lev] * step_x + west(coef[EB + lev] * step_x))
                new = new + (coef[NA + lev] * step_y + south(coef[NB + lev] * step_y))
                if lev < LEV - 1:
                    vertical = coef[BK + lev] * (ext[p + 1] - v)
                    new = new + vertical
                if above is not None:
                    new = new - above
                above = vertical
                ext[p] = new

    def advance():
        for f in range(2):
            above = None
            for lev in range(LEV):
                p = TRC + LEV * f + lev
                v = ext[p]
                flux_x = coef[EA + lev] * v + coef[EB + lev] * east(v)
                flux_y = coef[NA + lev] * v + coef[NB + lev] * north(v)
                new = v - (flux_x - west(flux_x)) - (flux_y - south(flux_y))
                if lev < LEV - 1:
                    below = coef[BK + lev] * (v - ext[p + 1])
                    new = new - below
                if above is not None:
                    new = new + above
                above = below
                if lev == 0:
                    new = new + force[f]
                ext[p] = new

    for f in range(2):
        ssum[f] = ext[COT + LEV * f, 0:ROWS, 0:COLS]

    @pl.loop(0, STEPS - 1)
    def _(step):
        retreat()
        for f in range(2):
            ssum[f] = ssum[f] + ext[COT + LEV * f, 0:ROWS, 0:COLS]

    mask0 = ext[MSK, 0:ROWS, 0:COLS]
    for f in range(2):
        surface = ssum[f] * mask0
        for h in range(2):
            s_all[lon, pl.ds(2 * h + f, ROWS, stride=4), :] = surface[:, 128 * h : 128 * h + 128]

    ssem = (s_ssem, s_rsem)
    mine = s_all.at[lon]
    row_blocks = s_all.at[pl.ds(4 * plane, 4)]
    near = [remote(mine, mine, ssem, b - 1, in_plane(b)) for b in range(1, 4)]
    far = [remote(row_blocks, row_blocks, ssem, 2 + a, across(a)) for a in range(1, 4)]
    for copy in near:
        copy.start()

    pl.loop(0, 4, unroll=4)(partial)

    for copy in near:
        copy.wait_recv()
    far[0].start()
    far[2].start()

    for g in range(16 // 2):
        first, second = (source(BATCH * PLANE_ORDER[2 * g // BATCH] + 2 * g % BATCH + i) for i in range(2))
        pick = jnp.concatenate([ids[pl.ds(first, 1), 0:CAP], ids[pl.ds(second, 1), 0:CAP]], axis=1)
        hot[:, 128 * g : 128 * g + 128] = (pick == iota((ATM, 128), 0)).astype(BF16)

    retreat()
    adjoint_out = pltpu.make_async_copy(ext.at[COT : COT + 8, 0:ROWS, 0:COLS], out_c, out_sem.at[0])
    adjoint_out.start()

    def gather(batch):
        count = BATCH * CAP
        terms = [split(z_rows[pl.ds(2 * count * batch + f, count, stride=2), :]) for f in range(2)]
        rhs = jnp.concatenate([jnp.concatenate([t[i] for t in terms], axis=1) for i in range(2)], axis=0)
        chosen = hot[:, count * batch : count * (batch + 1)]
        part = dot(jnp.concatenate([chosen, chosen], axis=1), rhs)
        for f in range(2):
            grad[f] = part[:, 128 * f : 128 * f + 128] + (grad[f] if batch else 0.0)

    def reverse(batch):
        for i in range(BATCH):
            hi, lo = split(s_all[source(BATCH * PLANE_ORDER[batch] + i)])
            v_cat[MSG * i : MSG * i + MSG, 0:128] = hi
            v_cat[MSG * i : MSG * i + MSG, 128:256] = hi
            v_cat[MSG * (BATCH + i) : MSG * (BATCH + i + 1), 0:128] = lo
            v_cat[MSG * (BATCH + i) : MSG * (BATCH + i + 1), 128:256] = lo
        size = MSG * BATCH

        @pl.loop(0, WB // 2, unroll=16)
        def _(pair):
            both = w_rev[pair]
            out = dot(v_cat[0:size], both) + dot(v_cat[size:], both)
            at = pl.multiple_of(pair * (2 * size), 2 * size)
            table_r[pl.ds(at, size), :] = out[:, 0:128]
            table_r[pl.ds(at + size, size), :] = out[:, 128:256]

        if batch:
            gather(batch - 1)

        @pl.loop(0, BATCH, unroll=4)
        def _(i):
            k = source(BATCH * PLANE_ORDER[batch] + i)
            base = pl.multiple_of((batch * BATCH + i) * (2 * CAP), 2 * CAP)
            for s in range(CAP):
                at = rows_s[1, k, s] + i * MSG
                z_rows[pl.ds(base + 2 * s, 2), :] = table_r[pl.ds(at, 2), :]


    for copy in partials:
        copy.wait_recv()
    for b in range(4):
        q_send[b] = (p_send[b] + p_recv[4 + b]) + (p_recv[8 + b] + p_recv[12 + b])
    sums = [remote(q_send.at[b], q_recv.at[b], psem, 2 + b, in_plane(b)) for b in range(1, 4)]
    for copy in sums:
        copy.start()
    reverse(0)
    far[1].start()
    total = q_send[0]
    for b in range(1, 4):
        sums[b - 1].wait_recv()
        total = total + q_recv[b]
    q_send[0] = total
    for f in range(2):
        for h in range(2):
            part = q_send[0, pl.ds(2 * h + f, ROWS, stride=4), :]
            force[f, 0:ROWS, 128 * h : 128 * h + 128] = part * mask0[:, 128 * h : 128 * h + 128]
        fsend_r[f] = force[f, 0:ROWS, 0:COLS]

    fsem = (f_send, f_recv)

    def put_f(r, tile, value):
        fsend_c[r : r + 8, :] = value

    pack_columns(lambda p: lambda r, c: force[p, r : r + 8, c : c + 128], 2, put_f)
    fcopies = [
        remote(fsend_r.at[:, 8:16], frecv_s, fsem, 0, (up, lon)),
        remote(fsend_r.at[:, 0:8], frecv_n, fsem, 1, (down, lon)),
    ] + column_copies(fsend_c, frecv_e, frecv_w, frecv_d, fsem, 2)
    for copy in fcopies:
        copy.start()

    far[PLANE_ORDER[1] - 1].wait_recv()
    reverse(1)
    far[PLANE_ORDER[2] - 1].wait_recv()
    reverse(2)
    far[PLANE_ORDER[3] - 1].wait_recv()
    reverse(3)

    for copy in fcopies:
        copy.wait_recv()
    for f in range(2):
        force[f, 16:24, 0:COLS] = jnp.where(low, frecv_n[f], frecv_s[f]) * edge_row2

    def put_force(p, r, value):
        force[p, r : r + 8, 256:384] = value * edge_row if r == 16 else value

    unpack_columns(frecv_e, frecv_w, frecv_d, 2, put_force)

    @pl.loop(0, STEPS)
    def _(step):
        advance()

    tracer_out = pltpu.make_async_copy(ext.at[TRC : TRC + 8, 0:ROWS, 0:COLS], out_t, out_sem.at[1])
    tracer_out.start()

    gather(3)
    grad_out = pltpu.make_async_copy(grad, out_g, out_sem.at[2])
    grad_out.start()

    for copy in halos + fcopies + near + far + partials + sums:
        copy.wait_send()
    adjoint_out.wait()
    tracer_out.wait()
    grad_out.wait()


def place(a, b, c, out_a, out_b, out_c, sem):
    copies = [pltpu.make_async_copy(x, y, sem.at[i]) for i, (x, y) in enumerate(((a, out_a), (b, out_b), (c, out_c)))]
    for copy in copies:
        copy.start()
    for copy in copies:
        copy.wait()


def on_device(n_lat, n_lon, tracers, cotangent, land_mask, diffusion, velocity, weights, atm_state, margins):
    fields = (2 * LEV, ROWS, COLS)
    margins = margins.reshape(3, n_lon, CAP)
    anywhere = pl.BlockSpec(memory_space=pltpu.HBM)

    def buf(*shape, dtype=F32):
        return pltpu.VMEM(shape, dtype)

    dma = pltpu.SemaphoreType.DMA
    scratch = [
        buf(PLANES, XROWS, XCOLS), buf(LEV, ROWS, COLS, dtype=jnp.int32), buf(2, ATM, BLOCK), buf(WB, BLOCK, BLOCK),
        pltpu.SMEM((2, n_lon, 128), jnp.int32), buf(2, n_lon, 128, dtype=jnp.int32), buf(3, n_lon, CAP, dtype=jnp.int32),
        buf(20, XROWS, XCOLS), buf(2, XROWS, XCOLS), buf(2, ROWS, COLS),
        buf(HALF, 8, COLS), buf(HALF, 8, COLS), buf(ROWS, 384), buf(HALF, 8, COLS), buf(HALF, 8, COLS),
        buf(ROWS, 384), buf(ROWS, 384), buf(4, 8, 384),
        buf(2, ROWS, COLS), buf(ROWS, 128), buf(2, 8, COLS), buf(2, 8, COLS),
        buf(ROWS, 128), buf(ROWS, 128), buf(4, 8, 128),
        buf(WB // 2, 256, 256, dtype=BF16), buf(WB // 2, 256, 256, dtype=BF16), buf(2 * ATM, BLOCK),
        buf(4 * ATM, 256, dtype=BF16), buf(WB * 2 * ATM, BLOCK), buf(2 * CAP, BLOCK),
        buf(n_lon, MSG, BLOCK), buf(n_lon, MSG, BLOCK), buf(4, MSG, BLOCK), buf(4, MSG, BLOCK),
        buf(n_lon, MSG, BLOCK), buf(2 * BATCH * MSG, 256, dtype=BF16), buf(WB * BATCH * MSG, BLOCK),
        buf(n_lon * 2 * CAP, BLOCK), buf(16, 128, dtype=jnp.int32),
        buf(ATM, n_lon * CAP, dtype=BF16), buf(n_lon, OCN, 2 * CAP, dtype=BF16), buf(2, ATM, BLOCK),
        dma((9,)), dma((8,)), dma((8,)), dma((6,)), dma((6,)), dma((6,)), dma((6,)), dma((8,)), dma((8,)), dma((3,)),
    ]

    def body(*refs):
        kernel(n_lat, n_lon, *refs)

    out_t, out_c, out_g = pl.pallas_call(
        body,
        out_shape=(
            jax.ShapeDtypeStruct(fields, F32),
            jax.ShapeDtypeStruct(fields, F32),
            jax.ShapeDtypeStruct((2, ATM, BLOCK), F32),
        ),
        in_specs=[anywhere] * 8,
        out_specs=(anywhere, anywhere, anywhere),
        scratch_shapes=scratch,
        compiler_params=pltpu.CompilerParams(collective_id=0, has_side_effects=True, vmem_limit_bytes=48 << 20),
    )(*(pltpu.with_memory_space_constraint(x, pltpu.HBM) for x in (
        tracers.reshape(fields),
        cotangent.reshape(fields),
        land_mask,
        diffusion.reshape(3 * LEV, ROWS, COLS),
        velocity.reshape(fields),
        weights,
        atm_state.reshape(2, ATM, BLOCK),
        margins,
    )))
    out_t, out_c, out_g = pl.pallas_call(
        place,
        out_shape=(
            jax.ShapeDtypeStruct(fields, F32),
            jax.ShapeDtypeStruct(fields, F32),
            jax.ShapeDtypeStruct((2, ATM, BLOCK), F32),
        ),
        in_specs=[pl.BlockSpec(memory_space=pltpu.VMEM)] * 3,
        compiler_params=pltpu.CompilerParams(vmem_limit_bytes=2 << 20),
        out_specs=(anywhere,) * 3,
        scratch_shapes=[dma((3,))],
    )(out_t, out_c, out_g)
    return out_t.reshape(tracers.shape), out_c.reshape(tracers.shape), out_g.reshape(atm_state.shape)


def solution(mesh):
    n_lat, n_lon = mesh.shape["lat"], mesh.shape["lon"]

    def run(*args):
        return on_device(n_lat, n_lon, *args)

    return jax.shard_map(
        run,
        mesh=mesh,
        in_specs=(
            P(None, None, "lat", "lon"),
            P(None, None, "lat", "lon"),
            P(None, "lat", "lon"),
            P(None, None, "lat", "lon"),
            P(None, None, "lat", "lon"),
            P(),
            P(None, "lat", "lon", None),
            P(None, "lat", "lon", None, None),
        ),
        out_specs=(
            P(None, None, "lat", "lon"),
            P(None, None, "lat", "lon"),
            P(None, "lat", "lon", None),
        ),
        check_vma=False,
    )
```
